32 devices in a mesh: pipe: 4 (over x, core), tensor: 8 (over z, y).
Axes of the slice: x: 2, y: 2, z: 4, core: 2. Of those that a mesh axis runs over, the one named last changes fastest.
Arguments:
- hidden: bfloat16 [384, 8192], P('pipe', 'tensor'), may hold values from -64 to 64
- weight: bfloat16 [8192, 16384], P(None, ('pipe', 'tensor')), may hold values from -0.23201941 to 0.23201941
- targets: int32 [384], replicated, may hold values from 0 to 16383
- token_weight: float32 [384], replicated, may hold values from 0.1 to 1
Outputs:
- token_loss: float32 [384], P('pipe')
- hidden_grad: float32 [384, 8192], P('pipe', 'tensor')
The draws below stay inside these ranges and needn't reach their ends.
All inputs are finite; a program needn't handle non-finite values.
Results may differ from the reference program's by a relative error of at most 0.0029.
Values may be sent and summed in bfloat16 or wider, within the bound.
A program may use at most 128 MiB of HBM per device.

```python
import math
import jax
import jax.numpy as jnp

D = 8192
TOKENS = 384
VOCAB = 16384


scale_base = 3.0


def weight_table(key):
    key_entries = jax.random.fold_in(key, 11)
    key_columns = jax.random.fold_in(key, 12)
    entries = jnp.clip(jax.random.normal(key_entries, (D, VOCAB), jnp.float32), -5.0, 5.0)
    ramp = 0.87 + 0.26 * jnp.arange(VOCAB, dtype=jnp.float32) / VOCAB
    jitter = jax.random.uniform(key_columns, (VOCAB,), jnp.float32, 0.8, 1.2)
    column_scale = ramp * jitter * scale_base / math.sqrt(D)
    return (entries * column_scale[None, :]).astype(jnp.bfloat16)


def draw_weight(key, part):
    return weight_table(key)


def draw_hidden(key, part):
    key_rows = jax.random.fold_in(key, 21)
    base = jnp.clip(jax.random.normal(key_rows, (TOKENS, D), jnp.float32), -6.0, 6.0)
    return base.astype(jnp.bfloat16)


def set_ends(values, key, low, high):
    longest = values.shape.index(max(values.shape))
    spots = []
    for shift in (0, 1):
        where = [jax.random.randint(jax.random.fold_in(key, axis), (), 0, length) for axis, length in enumerate(values.shape)]
        where[longest] = (where[longest] + shift) % values.shape[longest]
        spots.append(tuple(where))
    return values.at[spots[0]].set(low).at[spots[1]].set(high)


def setup_inputs(seed: int = 0) -> dict:
    splits = jax.random.split(jax.random.key(seed), 5)
    hidden = draw_hidden(jax.random.fold_in(splits[4], 71), 0)
    weight = draw_weight(jax.random.fold_in(splits[4], 71), 0)
    targets = set_ends(jax.random.randint(splits[2], (TOKENS,), 0, VOCAB), jax.random.fold_in(splits[2], 1), 0, VOCAB - 1).astype(jnp.int32)
    token_weight = jnp.clip(jnp.exp(jax.random.uniform(splits[3], (TOKENS,), jnp.float32, math.log(0.1), math.log(1.0))), 0.1, 1.0)
    return dict(hidden=hidden, weight=weight, targets=targets, token_weight=token_weight)


loss_scale = 32.0


def reference(hidden, weight, targets, token_weight):
    logits = jnp.dot(hidden, weight, preferred_element_type=jnp.float32)
    global_peak = jnp.max(logits, axis=1)
    global_total = jnp.sum(jnp.exp(logits - global_peak[:, None]), axis=1)
    log_total = global_peak + jnp.log(global_total)
    columns = jnp.arange(VOCAB, dtype=jnp.int32)
    target_hit = targets[:, None] == columns[None, :]
    target_logit = jnp.sum(jnp.where(target_hit, logits, jnp.float32(0.0)), axis=1)
    token_loss = log_total - target_logit
    softmax = jnp.exp(logits - log_total[:, None])
    onehot = target_hit.astype(jnp.float32)
    dlogits = (loss_scale * token_weight[:, None] * (softmax - onehot)).astype(jnp.bfloat16)
    hidden_grad = jnp.dot(dlogits, weight.T, preferred_element_type=jnp.float32)
    return token_loss, hidden_grad
```

```python
import functools

import jax
import jax.numpy as jnp
from jax import lax
from jax.experimental import pallas as pl
from jax.experimental.pallas import tpu as pltpu
from jax.sharding import PartitionSpec as P

loss_scale = 32.0
f32, bf16 = jnp.float32, jnp.bfloat16
MESH = pl.DeviceIdType.MESH


def flat_rows(block):
    n, rows, width = block.shape
    if rows % 16:
        return block.astype(f32).reshape(n * rows, width).astype(bf16)
    return block.reshape(n * rows, width)


def to_column(row):
    return jnp.transpose(jnp.broadcast_to(row, (128, row.shape[1])))[:, :1]


def kernel(
    nA, nB, nC, nH,
    hidden, weight, targets, token_weight,
    loss_out, grad_out,
    H, W, WT, acc, dl, Pb, Sib, b1, r1, b2, r2, zb, zr, keep, stb, st, lossb, tbuf, wbuf,
    lsem, hsem, osem, sends, g1, gd, gs, gz, rz, ssem,
):
    rows, cols = hidden.shape
    chunk = rows // nH
    half = cols // 2
    nP, nT = nA * 2, nB * nC
    lo, hi = pl.ds(0, half), pl.ds(half, half)
    p, t = lax.axis_index("pipe"), lax.axis_index("tensor")
    a, c = p // 2, lax.rem(p, 2)
    b, z = lax.rem(t, nB), t // nB

    def at(a_=None, b_=None, z_=None, c_=None):
        a_, b_ = (a if a_ is None else a_), (b if b_ is None else b_)
        z_, c_ = (z if z_ is None else z_), (c if c_ is None else c_)
        return {"pipe": a_ * 2 + c_, "tensor": z_ * nB + b_}

    left, right = z, nC - 1 - z
    both = jnp.minimum(left, right)
    longer = jnp.where(left > right, -1, 1)

    def near(i):
        d = (i + 1) // 2
        turn = jnp.where(lax.rem(i, 2) == 1, -d, d)
        return z + jnp.where(i <= 2 * both, turn, longer * (i - both))

    As = [lax.rem(a + o, nA) for o in range(1, nA)]
    Bs = [lax.rem(b + o, nB) for o in range(1, nB)]
    Zs = [near(jnp.int32(i)) for i in range(1, nC)]
    sib = at(c_=1 - c)
    Everyone = [
        at(a_=a_, b_=b_, c_=c_, z_=z_)
        for z_ in [z] + Zs for a_ in [a] + As for b_ in [b] + Bs for c_ in (c, 1 - c)
    ][1:]
    peers = Everyone[: nP * nB - 1] + [at(z_=k) for k in Zs]

    def put(src, dst, send, recv, dev):
        pltpu.make_async_remote_copy(
            src_ref=src, dst_ref=dst, send_sem=sends.at[send], recv_sem=recv,
            device_id=dev, device_id_type=MESH,
        ).start()

    def got(dst, recv):
        pltpu.make_async_remote_copy(
            src_ref=dst, dst_ref=dst, send_sem=sends.at[0], recv_sem=recv,
            device_id=sib, device_id_type=MESH,
        ).wait_recv()

    def sent(src, send):
        pltpu.make_async_remote_copy(
            src_ref=src, dst_ref=src, send_sem=sends.at[send], recv_sem=rz.at[0],
            device_id=sib, device_id_type=MESH,
        ).wait_send()

    barrier = pltpu.get_barrier_semaphore()
    for dev in peers:
        pl.semaphore_signal(barrier, inc=1, device_id=dev, device_id_type=MESH)

    def where(h, k, b_, a_, c_=None):
        return (h * nT + k * nB + b_) * nP + a_ * 2 + (c if c_ is None else c_)

    def slot(h, k, b_, a_):
        return H.at[where(h, k, b_, a_)]

    def blocks(n):
        return H.at[pl.ds(0, n)]

    hcopies = [
        pltpu.make_async_copy(
            hidden.at[pl.ds(h * chunk, chunk)], slot(h, z, b, a), hsem.at[h]
        )
        for h in range(nH)
    ]
    tcopy = pltpu.make_async_copy(targets, tbuf, lsem.at[1])
    kcopy = pltpu.make_async_copy(token_weight, wbuf, lsem.at[2])
    wcopy = pltpu.make_async_copy(weight, W, lsem.at[0])

    def own_plane(h):
        src, own = hidden.at[pl.ds(h * chunk, chunk)], slot(h, z, b, a)
        for j in As:
            put(src, own, 0, g1.at[h, z], at(a_=j))
        for j in Bs:
            put(src, own, 0, g1.at[h, z], at(b_=j))
        put(src, own, 0, gs.at[h, z], sib)

    def own_line(h, group):
        src, own = hidden.at[pl.ds(h * chunk, chunk)], slot(h, z, b, a)
        for k in (Zs, Zs[:2], Zs[2:])[group]:
            put(src, own, 0, gz.at[h, z], at(z_=k))

    def turn(n):
        WT[n] = jnp.transpose(W[n])

    def turns(first_, last_):
        for n in range(first_, last_):
            turn(n)

    def diagonal(h, k):
        for j in As:
            for m in Bs:
                ref = slot(h, k, b, j).at[:, lo]
                put(ref, ref, 0, gd.at[h, k], at(b_=m))
        for j in Bs:
            for m in As:
                ref = slot(h, k, j, a).at[:, hi]
                put(ref, ref, 0, gd.at[h, k], at(a_=m))

    def sibling(h, k, places):
        for b_, a_ in places:
            put(slot(h, k, b_, a_), slot(h, k, b_, a_), 0, gs.at[h, k], sib)

    beside = [(b, j) for j in As] + [(j, a) for j in Bs]
    across = [(m, j) for j in As for m in Bs]

    def own_forward(h):
        got(blocks(len(beside)), g1.at[h, z])
        diagonal(h, z)
        sibling(h, z, beside)

    def own_finish(h):
        got(blocks(len(across)), gd.at[h, z])
        sibling(h, z, across)

    def far(step):
        return step // (nC - 1), near(lax.rem(step, nC - 1) + 1)

    def spread(step):
        h, k = far(step)
        own = slot(h, k, b, a)
        got(own, gz.at[h, k])
        for j in As:
            put(own, own, 0, g1.at[h, k], at(a_=j))
        for j in Bs:
            put(own, own, 0, g1.at[h, k], at(b_=j))
        put(own, own, 0, gs.at[h, k], sib)

    def forward(step):
        h, k = far(step)
        got(blocks(len(beside)), g1.at[h, k])
        diagonal(h, k)
        sibling(h, k, beside)

    def finish(step):
        h, k = far(step)
        got(blocks(len(across)), gd.at[h, k])
        sibling(h, k, across)

    def product(h, k):
        got(blocks(nA * nB), gs.at[h, k])
        for b_ in range(nB):
            tt = k * nB + b_
            lhs = flat_rows(H[pl.ds((h * nT + tt) * nP, nP)])
            acc[h] += jnp.dot(lhs, W[tt], preferred_element_type=f32)

    def multiply(step):
        product(*far(step))

    def own_multiply(h):
        hcopies[h].wait()
        product(h, z)

    tokens, width = acc.shape[1:]
    padded = stb.shape[-1]
    device_block = p * lax.axis_size("tensor") + t
    def of_chunk(column, h):
        return column.reshape(nP, nH, chunk, 1)[:, h].reshape(nP * chunk, 1)

    def hits(h):
        columns = device_block * width + lax.broadcasted_iota(jnp.int32, (tokens, width), 1)
        return of_chunk(target_col, h) == columns

    def stats_local(h):
        logits = acc[h]
        peak = jnp.max(logits, axis=1, keepdims=True)
        total = jnp.sum(jnp.exp(logits - peak), axis=1, keepdims=True)
        chosen = jnp.sum(jnp.where(hits(h), logits, 0.0), axis=1, keepdims=True)
        lane = lax.broadcasted_iota(jnp.int32, (tokens, 128), 1)
        packed = jnp.where(
            lane == 0, peak, jnp.where(lane == 1, total, jnp.where(lane == 2, chosen, 0.0))
        )
        if padded > tokens:
            packed = jnp.concatenate([packed, jnp.zeros((padded - tokens, 128), f32)], axis=0)
        stb[h] = jnp.transpose(packed)[0:8]
        for dev in Everyone:
            put(stb.at[h, pl.ds(0, 4)], st.at[h, device_block], 5, ssem.at[h], dev)
        st[h, device_block] = stb[h, 0:4]

    def stats_line(h):
        got(st.at[h, pl.ds(0, len(Everyone))], ssem.at[h])
        peaks, totals, chosen = (st[h, :, n : n + 1].reshape(len(Everyone) + 1, padded) for n in range(3))
        peak = jnp.max(peaks, axis=0, keepdims=True)
        total = jnp.sum(totals * jnp.exp(peaks - peak), axis=0, keepdims=True)
        picked = jnp.sum(chosen, axis=0, keepdims=True)
        log_total = peak + jnp.log(total)
        loss = jnp.broadcast_to(log_total - picked, (8, padded))
        lossb[h] = pltpu.roll(loss, lax.rem((h - p) * chunk + nP * padded, padded), axis=1)
        softmax = jnp.exp(acc[h] - to_column(log_total)[:tokens])
        dl[h] = (of_chunk(scale_col, h) * (softmax - hits(h).astype(f32))).astype(bf16)

    def order(step):
        return step // nC, near(nC - 1 - lax.rem(step, nC))

    def produce(step):
        h, k = order(step)
        for b_ in range(nB):
            tt = k * nB + b_
            for part in (pl.ds(0, cols // 2), pl.ds(cols // 2, cols // 2)):
                term = jnp.dot(dl[h], WT[tt, :, part], preferred_element_type=f32)
                Pb[h, tt, :, :, :, part] = term.reshape(nA, 2, chunk, cols // 2)
            put(Pb.at[h, tt, :, 1 - c], Sib.at[h, tt], 1, gs.at[h, k], sib)

    def stage1(step):
        h, k = order(step)
        got(Sib.at[h, pl.ds(0, nB)], gs.at[h, k])
        for b_ in range(nB):
            for a_ in range(nA):
                Sib[h, k * nB + b_, a_] = Sib[h, k * nB + b_, a_] + Pb[h, k * nB + b_, a_, c]
        for o in range(1, nA):
            at_, to = (o - 1) * nB, (nA - o - 1) * nB
            for b_ in range(nB):
                b1[h, k, at_ + b_] = Sib[h, k * nB + b_, As[o - 1], :, lo].astype(bf16)
            put(
                b1.at[h, k, pl.ds(at_, nB)], r1.at[h, k, pl.ds(to, nB)],
                2, g1.at[h, k], at(a_=As[o - 1]),
            )
        for o in range(1, nB):
            at_, to = base + (o - 1) * nA, base + (nB - o - 1) * nA
            for a_ in range(nA):
                b1[h, k, at_ + a_] = Sib[h, k * nB + Bs[o - 1], a_, :, hi].astype(bf16)
            put(
                b1.at[h, k, pl.ds(at_, nA)], r1.at[h, k, pl.ds(to, nA)],
                2, g1.at[h, k], at(b_=Bs[o - 1]),
            )

    base, turned = (nA - 1) * nB, nB - 1

    def from_x(h, k, j):
        return sum(r1[h, k, m * nB + j].astype(f32) for m in range(nA - 1))

    def from_y(h, k, j):
        return sum(r1[h, k, base + m * nA + j].astype(f32) for m in range(nB - 1))

    def stage2(step):
        h, k = order(step)
        tb = k * nB + b
        got(r1.at[h, k], g1.at[h, k])
        for o in range(1, nB):
            j = Bs[o - 1]
            b2[h, k, o - 1] = (Sib[h, k * nB + j, a, :, lo] + from_x(h, k, j)).astype(bf16)
            put(b2.at[h, k, o - 1], r2.at[h, k, nB - o - 1], 3, gd.at[h, k], at(b_=j))
        for o in range(1, nA):
            j = As[o - 1]
            b2[h, k, turned + o - 1] = (Sib[h, tb, j, :, hi] + from_y(h, k, j)).astype(bf16)
            put(
                b2.at[h, k, turned + o - 1], r2.at[h, k, turned + nA - o - 1],
                3, gd.at[h, k], at(a_=j),
            )
        Sib[h, tb, a, :, lo] = Sib[h, tb, a, :, lo] + from_x(h, k, b)
        Sib[h, tb, a, :, hi] = Sib[h, tb, a, :, hi] + from_y(h, k, a)

    def stage3(step):
        h, k = order(step)
        tb = k * nB + b
        got(r2.at[h, k], gd.at[h, k])
        low = Sib[h, tb, a, :, lo] + sum(r2[h, k, m].astype(f32) for m in range(turned))
        high = Sib[h, tb, a, :, hi] + sum(
            r2[h, k, turned + m].astype(f32) for m in range(nA - 1)
        )

        @pl.when(k != z)
        def _():
            zb[h, k, :, lo] = low.astype(bf16)
            zb[h, k, :, hi] = high.astype(bf16)
            put(zb.at[h, k], zr.at[h, z], 4, rz.at[h], at(z_=k))

        @pl.when(k == z)
        def _():
            keep[h, :, lo] = low
            keep[h, :, hi] = high

    def complete(h):
        got(zr.at[h, pl.ds(0, nC - 1)], rz.at[h])
        keep[h] = keep[h] + sum(zr[h, k].astype(f32) for k in Zs)
        pltpu.make_async_copy(keep.at[h], grad_out.at[pl.ds(h * chunk, chunk)], osem.at[h]).start()

    nF, nS = nH * (nC - 1), nH * nC
    B = 2 if nH > 1 else 0
    o2 = 2
    c0 = B + nC - 2 + 2 + 2 + 0
    begin = c0 + 2
    comm, work, stats, back = [], [], [], []
    add = lambda to, when, action, *args: to.append((when, None, action, args))
    own = lambda h: h if h < 2 else o2 + (h - 2) * nC
    for h in range(2, nH):
        add(comm, own(h) - 2, own_plane, h)
    for h in range(nH):
        add(comm, own(h), own_forward, h)
    for h in range(1, nH):
        add(comm, 1 + (h - 1) * 4, own_line, h, 0)
    comm.append((B, nF, spread, ()))
    comm.append((B + 2, nF, forward, ()))
    for h in range(nH):
        add(comm, own(h) + 2, own_finish, h)
    comm.append((B + 2 + 2, nF, finish, ()))
    for h in range(nH):
        add(work, own(h) + 2 + 1, own_multiply, h)
    work.append((B + 2 + 2 + 0, nF, multiply, ()))
    turning = [(1, nT, turn, ())]
    add(comm, 0, wcopy.wait)
    for h in range(nH):
        w = c0 + h * (nC - 1)
        add(stats, w + 2 + (h * 2) // 2, stats_line, h)
        add(work, w, stats_local, h)
    back += [(begin + 1, nS, stage1, ()), (begin + 1 + 2, nS, stage2, ()), (begin + 1 + 2 + 2, nS, stage3, ()), (begin, nS, produce, ())]
    end = 1 + 2 + 2
    for h in range(nH):
        add(back, begin + (h + 1) * nC - 1 + end + (2 if h < nH - 1 else 0), complete, h)
    plans = [comm, turning, stats, back, work]
    length = begin + nS + end

    with jax.named_scope("barrier"):
        pl.semaphore_wait(barrier, len(peers))
    own_plane(0)
    own_line(0, 0)
    for copy in [tcopy, kcopy] + hcopies + [wcopy]:
        copy.start()
    with jax.named_scope("zero"):
        acc[...] = jnp.zeros_like(acc)
        tcopy.wait()
        kcopy.wait()
        target_col = to_column(tbuf[...].reshape(1, -1).astype(f32)).astype(jnp.int32)
        scale_col = loss_scale * to_column(wbuf[...].reshape(1, -1))
    if nH > 1:
        own_plane(1)

    def during(i, begin, count, action):
        @pl.when((i >= begin) & (i < begin + count))
        def _():
            with jax.named_scope(action.__name__):
                action(i - begin)

    def once(i, when, action, *args):
        @pl.when(i == when)
        def _():
            with jax.named_scope(action.__name__):
                action(*args)

    def step(i, carry):
        for entries in plans:
            first_i = min(e[0] for e in entries)
            last_i = max(e[0] + (e[1] or 1) for e in entries)

            @pl.when((i >= first_i) & (i < last_i))
            def _():
                for when, count, action, args in entries:
                    if count is None:
                        once(i, when, action, *args)
                    else:
                        during(i, when, count, action)
        return carry

    lax.fori_loop(0, length, step, 0)
    with jax.named_scope("loss"):
        lane = lax.broadcasted_iota(jnp.int32, (8, padded), 1)
        loss = lossb[0]
        for h in range(1, nH):
            loss = jnp.where(lane >= h * chunk, lossb[h], loss)
        loss_out[...] = loss[0, :rows]

    with jax.named_scope('drain'):
        sent(blocks(nH * (nT * nP - 1)), 0)
        sent(Sib, 1)
        sent(b1, 2)
        sent(b2, 3)
        sent(zb.at[:, pl.ds(0, nC - 1)], 4)
        sent(st.at[:, pl.ds(0, len(Everyone))], 5)
        for h in range(nH):
            pltpu.make_async_copy(keep.at[h], grad_out.at[pl.ds(h * chunk, chunk)], osem.at[h]).wait()


def local(hidden, weight, targets, token_weight):
    rows, cols = hidden.shape
    n_pipe, n_tensor = lax.axis_size("pipe"), lax.axis_size("tensor")
    nA, nB, nC = n_pipe // 2, 2, n_tensor // 2
    tokens, width = targets.shape[0], weight.shape[1]
    vmem, dma = pltpu.VMEM, pltpu.SemaphoreType.DMA
    nH = 3 if rows % (16 * 3) == 0 else 1
    chunk = rows // nH
    half = cols // 2
    n1, n2 = (nA - 1) * nB + (nB - 1) * nA, nB + nA - 2
    part = n_pipe * chunk
    padded = -(-part // 128) * 128
    token_loss, hidden_grad = pl.pallas_call(
        functools.partial(kernel, nA, nB, nC, nH),
        out_shape=(
            jax.ShapeDtypeStruct((rows,), f32),
            jax.ShapeDtypeStruct((rows, cols), f32),
        ),
        in_specs=[pl.BlockSpec(memory_space=pl.ANY)] * 4,
        out_specs=[pl.BlockSpec(memory_space=vmem), pl.BlockSpec(memory_space=pl.ANY)],
        scratch_shapes=[
            vmem((nH * n_tensor * n_pipe, chunk, cols), bf16),
            vmem((n_tensor, cols, width), bf16),
            vmem((n_tensor, width, cols), bf16),
            vmem((nH, part, width), f32),
            vmem((nH, part, width), bf16),
            vmem((nH, n_tensor, nA, 2, chunk, cols), f32),
            vmem((nH, n_tensor, nA, chunk, cols), f32),
            vmem((nH, nC, n1, chunk, half), bf16),
            vmem((nH, nC, n1, chunk, half), bf16),
            vmem((nH, nC, n2, chunk, half), bf16),
            vmem((nH, nC, n2, chunk, half), bf16),
            vmem((nH, nC, chunk, cols), bf16),
            vmem((nH, nC, chunk, cols), bf16),
            vmem((nH, chunk, cols), f32),
            vmem((nH, 8, padded), f32),
            vmem((nH, n_pipe * n_tensor, 4, padded), f32),
            vmem((nH, 8, padded), f32),
            vmem((tokens,), jnp.int32),
            vmem((tokens,), f32),
            dma((3,)),
            dma((nH,)),
            dma((nH,)),
            dma((6,)),
            dma((nH, nC)),
            dma((nH, nC)),
            dma((nH, nC)),
            dma((nH, nC)),
            dma((nH,)),
            dma((nH,)),
        ],
        compiler_params=pltpu.CompilerParams(
            collective_id=0, has_side_effects=True, vmem_limit_bytes=62 * 1024 * 1024
        ),
    )(
        hidden,
        weight.reshape(n_tensor, cols, width),
        targets,
        token_weight,
    )
    return token_loss, hidden_grad


def solution(mesh):
    in_specs = (P("pipe", "tensor"), P(None, ("pipe", "tensor")), P(), P())
    out_specs = (P("pipe"), P("pipe", "tensor"))
    return jax.shard_map(local, mesh=mesh, in_specs=in_specs, out_specs=out_specs, check_vma=False)
```

```python
import functools

import jax
import jax.numpy as jnp
from jax import lax
from jax.experimental import pallas as pl
from jax.experimental.pallas import tpu as pltpu
from jax.sharding import PartitionSpec as P

loss_scale = 32.0
f32, bf16 = jnp.float32, jnp.bfloat16
MESH = pl.DeviceIdType.MESH


def flat_rows(block):
    n, rows, width = block.shape
    if rows % 16:
        return block.astype(f32).reshape(n * rows, width).astype(bf16)
    return block.reshape(n * rows, width)


def to_column(row):
    return jnp.transpose(jnp.broadcast_to(row, (128, row.shape[1])))[:, :1]


def kernel(
    nA, nB, nC, nH,
    hidden, weight, targets, token_weight,
    loss_out, grad_out,
    H, W, WT, acc, dl, Pb, Sib, b1, r1, b2, r2, zb, zr, keep, stb, st, lossb, lossrow, tbuf, wbuf,
    lsem, hsem, osem, sends, g1, gd, gs, gz, rz, ssem,
):
    rows, cols = hidden.shape
    chunk = rows // nH
    half = cols // 2
    nP, nT = nA * 2, nB * nC
    lo, hi = pl.ds(0, half), pl.ds(half, half)
    p, t = lax.axis_index("pipe"), lax.axis_index("tensor")
    a, c = p // 2, lax.rem(p, 2)
    b, z = lax.rem(t, nB), t // nB

    def at(a_=None, b_=None, z_=None, c_=None):
        a_, b_ = (a if a_ is None else a_), (b if b_ is None else b_)
        z_, c_ = (z if z_ is None else z_), (c if c_ is None else c_)
        return {"pipe": a_ * 2 + c_, "tensor": z_ * nB + b_}

    left, right = z, nC - 1 - z
    both = jnp.minimum(left, right)
    longer = jnp.where(left > right, -1, 1)

    def near(i):
        d = (i + 1) // 2
        turn = jnp.where(lax.rem(i, 2) == 1, -d, d)
        return z + jnp.where(i <= 2 * both, turn, longer * (i - both))

    As = [lax.rem(a + o, nA) for o in range(1, nA)]
    Bs = [lax.rem(b + o, nB) for o in range(1, nB)]
    Zs = [near(jnp.int32(i)) for i in range(1, nC)]
    sib = at(c_=1 - c)
    Everyone = [
        at(a_=a_, b_=b_, c_=c_, z_=z_)
        for z_ in [z] + Zs for a_ in [a] + As for b_ in [b] + Bs for c_ in (c, 1 - c)
    ][1:]
    peers = Everyone[: nP * nB - 1] + [at(z_=k) for k in Zs]

    def put(src, dst, send, recv, dev):
        pltpu.make_async_remote_copy(
            src_ref=src, dst_ref=dst, send_sem=sends.at[send], recv_sem=recv,
            device_id=dev, device_id_type=MESH,
        ).start()

    def got(dst, recv):
        pltpu.make_async_remote_copy(
            src_ref=dst, dst_ref=dst, send_sem=sends.at[0], recv_sem=recv,
            device_id=sib, device_id_type=MESH,
        ).wait_recv()

    def sent(src, send):
        pltpu.make_async_remote_copy(
            src_ref=src, dst_ref=src, send_sem=sends.at[send], recv_sem=rz.at[0],
            device_id=sib, device_id_type=MESH,
        ).wait_send()

    barrier = pltpu.get_barrier_semaphore()
    for dev in peers:
        pl.semaphore_signal(barrier, inc=1, device_id=dev, device_id_type=MESH)

    def where(h, k, b_, a_, c_=None):
        return (h * nT + k * nB + b_) * nP + a_ * 2 + (c if c_ is None else c_)

    def slot(h, k, b_, a_):
        return H.at[where(h, k, b_, a_)]

    def blocks(n):
        return H.at[pl.ds(0, n)]

    hcopies = [
        pltpu.make_async_copy(
            hidden.at[pl.ds(h * chunk, chunk)], slot(h, z, b, a), hsem.at[h]
        )
        for h in range(nH)
    ]
    tcopy = pltpu.make_async_copy(targets, tbuf, lsem.at[1])
    kcopy = pltpu.make_async_copy(token_weight, wbuf, lsem.at[2])
    wcopy = pltpu.make_async_copy(weight, W, lsem.at[0])

    def own_plane(h):
        src, own = hidden.at[pl.ds(h * chunk, chunk)], slot(h, z, b, a)
        for j in As:
            put(src, own, 0, g1.at[h, z], at(a_=j))
        for j in Bs:
            put(src, own, 0, g1.at[h, z], at(b_=j))
        put(src, own, 0, gs.at[h, z], sib)

    def own_line(h, group):
        src, own = hidden.at[pl.ds(h * chunk, chunk)], slot(h, z, b, a)
        for k in (Zs, Zs[:2], Zs[2:])[group]:
            put(src, own, 0, gz.at[h, z], at(z_=k))

    def turn(n):
        WT[n] = jnp.transpose(W[n])

    def turns(first_, last_):
        for n in range(first_, last_):
            turn(n)

    def diagonal(h, k):
        for j in As:
            for m in Bs:
                ref = slot(h, k, b, j).at[:, lo]
                put(ref, ref, 0, gd.at[h, k], at(b_=m))
        for j in Bs:
            for m in As:
                ref = slot(h, k, j, a).at[:, hi]
                put(ref, ref, 0, gd.at[h, k], at(a_=m))

    def sibling(h, k, places):
        for b_, a_ in places:
            put(slot(h, k, b_, a_), slot(h, k, b_, a_), 0, gs.at[h, k], sib)

    beside = [(b, j) for j in As] + [(j, a) for j in Bs]
    across = [(m, j) for j in As for m in Bs]

    def own_forward(h):
        got(blocks(len(beside)), g1.at[h, z])
        diagonal(h, z)
        sibling(h, z, beside)

    def own_finish(h):
        got(blocks(len(across)), gd.at[h, z])
        sibling(h, z, across)

    def far(step):
        return step // (nC - 1), near(lax.rem(step, nC - 1) + 1)

    def spread(step):
        h, k = far(step)
        own = slot(h, k, b, a)
        got(own, gz.at[h, k])
        for j in As:
            put(own, own, 0, g1.at[h, k], at(a_=j))
        for j in Bs:
            put(own, own, 0, g1.at[h, k], at(b_=j))
        put(own, own, 0, gs.at[h, k], sib)

    def forward(step):
        h, k = far(step)
        got(blocks(len(beside)), g1.at[h, k])
        diagonal(h, k)
        sibling(h, k, beside)

    def finish(step):
        h, k = far(step)
        got(blocks(len(across)), gd.at[h, k])
        sibling(h, k, across)

    def product(h, k):
        got(blocks(nA * nB), gs.at[h, k])
        for b_ in range(nB):
            tt = k * nB + b_
            lhs = flat_rows(H[pl.ds((h * nT + tt) * nP, nP)])
            acc[h] += jnp.dot(lhs, W[tt], preferred_element_type=f32)

    def multiply(step):
        product(*far(step))

    def own_multiply(h):
        hcopies[h].wait()
        product(h, z)

    tokens, width = acc.shape[1:]
    padded = stb.shape[-1]
    device_block = p * lax.axis_size("tensor") + t
    def of_chunk(column, h):
        return column.reshape(nP, nH, chunk, 1)[:, h].reshape(nP * chunk, 1)

    def hits(h):
        columns = device_block * width + lax.broadcasted_iota(jnp.int32, (tokens, width), 1)
        return of_chunk(target_col, h) == columns

    def stats_local(h):
        logits = acc[h]
        peak = jnp.max(logits, axis=1, keepdims=True)
        total = jnp.sum(jnp.exp(logits - peak), axis=1, keepdims=True)
        chosen = jnp.sum(jnp.where(hits(h), logits, 0.0), axis=1, keepdims=True)
        lane = lax.broadcasted_iota(jnp.int32, (tokens, 128), 1)
        packed = jnp.where(
            lane == 0, peak, jnp.where(lane == 1, total, jnp.where(lane == 2, chosen, 0.0))
        )
        if padded > tokens:
            packed = jnp.concatenate([packed, jnp.zeros((padded - tokens, 128), f32)], axis=0)
        stb[h] = jnp.transpose(packed)[0:8]
        for dev in Everyone:
            put(stb.at[h, pl.ds(0, 4)], st.at[h, device_block], 5, ssem.at[h], dev)
        st[h, device_block] = stb[h, 0:4]

    def stats_line(h):
        got(st.at[h, pl.ds(0, len(Everyone))], ssem.at[h])
        peaks, totals, chosen = (st[h, :, n : n + 1].reshape(len(Everyone) + 1, padded) for n in range(3))
        peak = jnp.max(peaks, axis=0, keepdims=True)
        total = jnp.sum(totals * jnp.exp(peaks - peak), axis=0, keepdims=True)
        picked = jnp.sum(chosen, axis=0, keepdims=True)
        log_total = peak + jnp.log(total)
        loss = jnp.broadcast_to(log_total - picked, (8, padded))
        lossb[h] = pltpu.roll(loss, lax.rem((h - p) * chunk + nP * padded, padded), axis=1)
        softmax = jnp.exp(acc[h] - to_column(log_total)[:tokens])
        dl[h] = (of_chunk(scale_col, h) * (softmax - hits(h).astype(f32))).astype(bf16)

    def order(step):
        return step // nC, near(nC - 1 - lax.rem(step, nC))

    def produce(step):
        h, k = order(step)
        for b_ in range(nB):
            tt = k * nB + b_
            for part in (pl.ds(0, cols // 2), pl.ds(cols // 2, cols // 2)):
                term = jnp.dot(dl[h], WT[tt, :, part], preferred_element_type=f32)
                Pb[h, tt, :, :, :, part] = term.reshape(nA, 2, chunk, cols // 2)
            put(Pb.at[h, tt, :, 1 - c], Sib.at[h, tt], 1, gs.at[h, k], sib)

    def stage1(step):
        h, k = order(step)
        got(Sib.at[h, pl.ds(0, nB)], gs.at[h, k])
        for b_ in range(nB):
            for a_ in range(nA):
                Sib[h, k * nB + b_, a_] = Sib[h, k * nB + b_, a_] + Pb[h, k * nB + b_, a_, c]
        for o in range(1, nA):
            at_, to = (o - 1) * nB, (nA - o - 1) * nB
            for b_ in range(nB):
                b1[h, k, at_ + b_] = Sib[h, k * nB + b_, As[o - 1], :, lo].astype(bf16)
            put(
                b1.at[h, k, pl.ds(at_, nB)], r1.at[h, k, pl.ds(to, nB)],
                2, g1.at[h, k], at(a_=As[o - 1]),
            )
        for o in range(1, nB):
            at_, to = base + (o - 1) * nA, base + (nB - o - 1) * nA
            for a_ in range(nA):
                b1[h, k, at_ + a_] = Sib[h, k * nB + Bs[o - 1], a_, :, hi].astype(bf16)
            put(
                b1.at[h, k, pl.ds(at_, nA)], r1.at[h, k, pl.ds(to, nA)],
                2, g1.at[h, k], at(b_=Bs[o - 1]),
            )

    base, turned = (nA - 1) * nB, nB - 1

    def from_x(h, k, j):
        return sum(r1[h, k, m * nB + j].astype(f32) for m in range(nA - 1))

    def from_y(h, k, j):
        return sum(r1[h, k, base + m * nA + j].astype(f32) for m in range(nB - 1))

    def stage2(step):
        h, k = order(step)
        tb = k * nB + b
        got(r1.at[h, k], g1.at[h, k])
        for o in range(1, nB):
            j = Bs[o - 1]
            b2[h, k, o - 1] = (Sib[h, k * nB + j, a, :, lo] + from_x(h, k, j)).astype(bf16)
            put(b2.at[h, k, o - 1], r2.at[h, k, nB - o - 1], 3, gd.at[h, k], at(b_=j))
        for o in range(1, nA):
            j = As[o - 1]
            b2[h, k, turned + o - 1] = (Sib[h, tb, j, :, hi] + from_y(h, k, j)).astype(bf16)
            put(
                b2.at[h, k, turned + o - 1], r2.at[h, k, turned + nA - o - 1],
                3, gd.at[h, k], at(a_=j),
            )
        Sib[h, tb, a, :, lo] = Sib[h, tb, a, :, lo] + from_x(h, k, b)
        Sib[h, tb, a, :, hi] = Sib[h, tb, a, :, hi] + from_y(h, k, a)

    def stage3(step):
        h, k = order(step)
        tb = k * nB + b
        got(r2.at[h, k], gd.at[h, k])
        low = Sib[h, tb, a, :, lo] + sum(r2[h, k, m].astype(f32) for m in range(turned))
        high = Sib[h, tb, a, :, hi] + sum(
            r2[h, k, turned + m].astype(f32) for m in range(nA - 1)
        )

        @pl.when(k != z)
        def _():
            zb[h, k, :, lo] = low.astype(bf16)
            zb[h, k, :, hi] = high.astype(bf16)
            put(zb.at[h, k], zr.at[h, z], 4, rz.at[h], at(z_=k))

        @pl.when(k == z)
        def _():
            keep[h, :, lo] = low
            keep[h, :, hi] = high

    def complete(h):
        got(zr.at[h, pl.ds(0, nC - 1)], rz.at[h])
        keep[h] = keep[h] + sum(zr[h, k].astype(f32) for k in Zs)
        pltpu.make_async_copy(keep.at[h], grad_out.at[pl.ds(h * chunk, chunk)], osem.at[h]).start()

    nF, nS = nH * (nC - 1), nH * nC
    B = 2 if nH > 1 else 0
    o2 = 2
    c0 = B + nC - 2 + 2 + 2 + 0
    begin = c0 + 2
    comm, work, stats, back = [], [], [], []
    add = lambda to, when, action, *args: to.append((when, None, action, args))
    own = lambda h: h if h < 2 else o2 + (h - 2) * nC
    for h in range(2, nH):
        if not False:
            add(comm, own(h) - 2, own_plane, h)
    for h in range(nH):
        add(comm, own(h), own_forward, h)
    for h in range(1, nH):
        add(comm, 2 + (h - 1) * 4, own_line, h, 0)
    comm.append((B, nF, spread, ()))
    comm.append((B + 2, nF, forward, ()))
    for h in range(nH):
        add(comm, own(h) + 2, own_finish, h)
    comm.append((B + 2 + 2, nF, finish, ()))
    for h in range(nH):
        add(work, own(h) + 2 + 1, own_multiply, h)
    work.append((B + 2 + 2 + 0, nF, multiply, ()))
    turning = [(1, nT, turn, ())]
    add(comm, 0, wcopy.wait)
    for h in range(nH):
        w = c0 + h * (nC - 1)
        add(stats, w + 2 + (h * 2) // 2, stats_line, h)
        add(work, w, stats_local, h)
    back += [(begin + 1, nS, stage1, ()), (begin + 1 + 2, nS, stage2, ()), (begin + 1 + 2 + 2, nS, stage3, ()), (begin, nS, produce, ())]
    end = 1 + 2 + 2
    for h in range(nH):
        add(back, begin + (h + 1) * nC - 1 + end + (2 if h < nH - 1 else 0), complete, h)
    plans = [comm, turning, stats, back, work]
    length = begin + nS + end

    with jax.named_scope("barrier"):
        pl.semaphore_wait(barrier, len(peers))
    own_plane(0)
    own_line(0, 0)
    for copy in [tcopy, kcopy] + hcopies + [wcopy]:
        copy.start()
    with jax.named_scope("zero"):
        acc[...] = jnp.zeros_like(acc)
        tcopy.wait()
        kcopy.wait()
        target_col = to_column(tbuf[...].reshape(1, -1).astype(f32)).astype(jnp.int32)
        scale_col = loss_scale * to_column(wbuf[...].reshape(1, -1))
    if nH > 1:
        own_plane(1)

    def during(i, begin, count, action):
        @pl.when((i >= begin) & (i < begin + count))
        def _():
            with jax.named_scope(action.__name__):
                action(i - begin)

    def once(i, when, action, *args):
        @pl.when(i == when)
        def _():
            with jax.named_scope(action.__name__):
                action(*args)

    def step(i, carry):
        for entries in plans:
            first_i = min(e[0] for e in entries)
            last_i = max(e[0] + (e[1] or 1) for e in entries)

            @pl.when((i >= first_i) & (i < last_i))
            def _():
                for when, count, action, args in entries:
                    if count is None:
                        once(i, when, action, *args)
                    else:
                        during(i, when, count, action)
        return carry

    lax.fori_loop(0, length, step, 0)
    with jax.named_scope("loss"):
        lane = lax.broadcasted_iota(jnp.int32, (8, padded), 1)
        loss = lossb[0]
        for h in range(1, nH):
            loss = jnp.where(lane >= h * chunk, lossb[h], loss)
        lossrow[...] = loss[0, :rows]
        lcopy = pltpu.make_async_copy(lossrow, loss_out, lsem.at[1])
        lcopy.start()

    with jax.named_scope('drain'):
        sent(blocks(nH * (nT * nP - 1)), 0)
        sent(Sib, 1)
        sent(b1, 2)
        sent(b2, 3)
        sent(zb.at[:, pl.ds(0, nC - 1)], 4)
        sent(st.at[:, pl.ds(0, len(Everyone))], 5)
        for h in range(nH):
            pltpu.make_async_copy(keep.at[h], grad_out.at[pl.ds(h * chunk, chunk)], osem.at[h]).wait()
        lcopy.wait()


def hand_over(loss, grad, loss_out, grad_out):
    loss_out[...] = loss[...]
    grad_out[...] = grad[...]


def local(hidden, weight, targets, token_weight):
    rows, cols = hidden.shape
    n_pipe, n_tensor = lax.axis_size("pipe"), lax.axis_size("tensor")
    nA, nB, nC = n_pipe // 2, 2, n_tensor // 2
    tokens, width = targets.shape[0], weight.shape[1]
    vmem, dma = pltpu.VMEM, pltpu.SemaphoreType.DMA
    nH = 3 if rows % (16 * 3) == 0 else 1
    chunk = rows // nH
    half = cols // 2
    n1, n2 = (nA - 1) * nB + (nB - 1) * nA, nB + nA - 2
    part = n_pipe * chunk
    padded = -(-part // 128) * 128
    token_loss, hidden_grad = pl.pallas_call(
        functools.partial(kernel, nA, nB, nC, nH),
        out_shape=(
            jax.ShapeDtypeStruct((rows,), f32),
            jax.ShapeDtypeStruct((rows, cols), f32),
        ),
        in_specs=[pl.BlockSpec(memory_space=pl.ANY)] * 4,
        out_specs=[pl.BlockSpec(memory_space=pl.ANY)] * 2,
        scratch_shapes=[
            vmem((nH * n_tensor * n_pipe, chunk, cols), bf16),
            vmem((n_tensor, cols, width), bf16),
            vmem((n_tensor, width, cols), bf16),
            vmem((nH, part, width), f32),
            vmem((nH, part, width), bf16),
            vmem((nH, n_tensor, nA, 2, chunk, cols), f32),
            vmem((nH, n_tensor, nA, chunk, cols), f32),
            vmem((nH, nC, n1, chunk, half), bf16),
            vmem((nH, nC, n1, chunk, half), bf16),
            vmem((nH, nC, n2, chunk, half), bf16),
            vmem((nH, nC, n2, chunk, half), bf16),
            vmem((nH, nC, chunk, cols), bf16),
            vmem((nH, nC, chunk, cols), bf16),
            vmem((nH, chunk, cols), f32),
            vmem((nH, 8, padded), f32),
            vmem((nH, n_pipe * n_tensor, 4, padded), f32),
            vmem((nH, 8, padded), f32),
            vmem((rows,), f32),
            vmem((tokens,), jnp.int32),
            vmem((tokens,), f32),
            dma((3,)),
            dma((nH,)),
            dma((nH,)),
            dma((6,)),
            dma((nH, nC)),
            dma((nH, nC)),
            dma((nH, nC)),
            dma((nH, nC)),
            dma((nH,)),
            dma((nH,)),
        ],
        compiler_params=pltpu.CompilerParams(
            collective_id=0, has_side_effects=True, vmem_limit_bytes=54 * 1024 * 1024
        ),
    )(
        hidden,
        weight.reshape(n_tensor, cols, width),
        targets,
        token_weight,
    )
    return pl.pallas_call(
        hand_over,
        out_shape=(
            jax.ShapeDtypeStruct((rows,), f32),
            jax.ShapeDtypeStruct((rows, cols), f32),
        ),
        in_specs=[pl.BlockSpec(memory_space=vmem)] * 2,
        out_specs=[pl.BlockSpec(memory_space=vmem)] * 2,
    )(token_loss, hidden_grad)


def solution(mesh):
    in_specs = (P("pipe", "tensor"), P(None, ("pipe", "tensor")), P(), P())
    out_specs = (P("pipe"), P("pipe", "tensor"))
    return jax.shard_map(local, mesh=mesh, in_specs=in_specs, out_specs=out_specs, check_vma=False)
```

```python
import functools

import jax
import jax.numpy as jnp
from jax import lax
from jax.experimental import pallas as pl
from jax.experimental.pallas import tpu as pltpu
from jax.sharding import PartitionSpec as P

loss_scale = 32.0
f32, bf16 = jnp.float32, jnp.bfloat16
MESH = pl.DeviceIdType.MESH


def flat_rows(block):
    n, rows, width = block.shape
    if rows % 16:
        return block.astype(f32).reshape(n * rows, width).astype(bf16)
    return block.reshape(n * rows, width)


def to_column(row):
    return jnp.transpose(jnp.broadcast_to(row, (128, row.shape[1])))[:, :1]


def kernel(
    nA, nB, nC, nH,
    hidden, weight, targets, token_weight,
    loss_out, grad_out,
    H, W, WT, acc, dl, Pb, Sib, b1, r1, b2, r2, zb, zr, keep, stb, st, lossb, lossrow, tbuf, wbuf,
    lsem, hsem, osem, sends, g1, gd, gs, gz, rz, ssem,
):
    rows, cols = hidden.shape
    chunk = rows // nH
    half = cols // 2
    nP, nT = nA * 2, nB * nC
    lo, hi = pl.ds(0, half), pl.ds(half, half)
    p, t = lax.axis_index("pipe"), lax.axis_index("tensor")
    a, c = p // 2, lax.rem(p, 2)
    b, z = lax.rem(t, nB), t // nB

    def at(a_=None, b_=None, z_=None, c_=None):
        a_, b_ = (a if a_ is None else a_), (b if b_ is None else b_)
        z_, c_ = (z if z_ is None else z_), (c if c_ is None else c_)
        return {"pipe": a_ * 2 + c_, "tensor": z_ * nB + b_}

    left, right = z, nC - 1 - z
    both = jnp.minimum(left, right)
    longer = jnp.where(left > right, -1, 1)

    def near(i):
        d = (i + 1) // 2
        turn = jnp.where(lax.rem(i, 2) == 1, -d, d)
        return z + jnp.where(i <= 2 * both, turn, longer * (i - both))

    As = [lax.rem(a + o, nA) for o in range(1, nA)]
    Bs = [lax.rem(b + o, nB) for o in range(1, nB)]
    Zs = [near(jnp.int32(i)) for i in range(1, nC)]
    sib = at(c_=1 - c)
    Everyone = [
        at(a_=a_, b_=b_, c_=c_, z_=z_)
        for z_ in [z] + Zs for a_ in [a] + As for b_ in [b] + Bs for c_ in (c, 1 - c)
    ][1:]
    peers = Everyone[: nP * nB - 1] + [at(z_=k) for k in Zs]

    def put(src, dst, send, recv, dev):
        pltpu.make_async_remote_copy(
            src_ref=src, dst_ref=dst, send_sem=sends.at[send], recv_sem=recv,
            device_id=dev, device_id_type=MESH,
        ).start()

    def got(dst, recv):
        pltpu.make_async_remote_copy(
            src_ref=dst, dst_ref=dst, send_sem=sends.at[0], recv_sem=recv,
            device_id=sib, device_id_type=MESH,
        ).wait_recv()

    def sent(src, send):
        pltpu.make_async_remote_copy(
            src_ref=src, dst_ref=src, send_sem=sends.at[send], recv_sem=rz.at[0],
            device_id=sib, device_id_type=MESH,
        ).wait_send()

    barrier = pltpu.get_barrier_semaphore()
    for dev in peers:
        pl.semaphore_signal(barrier, inc=1, device_id=dev, device_id_type=MESH)

    def where(h, k, b_, a_, c_=None):
        return (h * nT + k * nB + b_) * nP + a_ * 2 + (c if c_ is None else c_)

    def slot(h, k, b_, a_):
        return H.at[where(h, k, b_, a_)]

    def blocks(n):
        return H.at[pl.ds(0, n)]

    hcopies = [
        pltpu.make_async_copy(
            hidden.at[pl.ds(h * chunk, chunk)], slot(h, z, b, a), hsem.at[h]
        )
        for h in range(nH)
    ]
    tcopy = pltpu.make_async_copy(targets, tbuf, lsem.at[1])
    kcopy = pltpu.make_async_copy(token_weight, wbuf, lsem.at[2])
    wcopy = pltpu.make_async_copy(weight, W, lsem.at[0])

    def own_plane(h):
        src, own = hidden.at[pl.ds(h * chunk, chunk)], slot(h, z, b, a)
        for j in As:
            put(src, own, 0, g1.at[h, z], at(a_=j))
        for j in Bs:
            put(src, own, 0, g1.at[h, z], at(b_=j))
        put(src, own, 0, gs.at[h, z], sib)

    def own_line(h, group):
        src, own = hidden.at[pl.ds(h * chunk, chunk)], slot(h, z, b, a)
        for k in (Zs, Zs[:2], Zs[2:])[group]:
            put(src, own, 0, gz.at[h, z], at(z_=k))

    def turn(n):
        WT[n] = jnp.transpose(W[n])

    def turns(first_, last_):
        for n in range(first_, last_):
            turn(n)

    def diagonal(h, k):
        for j in As:
            for m in Bs:
                ref = slot(h, k, b, j).at[:, lo]
                put(ref, ref, 0, gd.at[h, k], at(b_=m))
        for j in Bs:
            for m in As:
                ref = slot(h, k, j, a).at[:, hi]
                put(ref, ref, 0, gd.at[h, k], at(a_=m))

    def sibling(h, k, places):
        for b_, a_ in places:
            put(slot(h, k, b_, a_), slot(h, k, b_, a_), 0, gs.at[h, k], sib)

    beside = [(b, j) for j in As] + [(j, a) for j in Bs]
    across = [(m, j) for j in As for m in Bs]

    def own_forward(h):
        got(blocks(len(beside)), g1.at[h, z])
        diagonal(h, z)
        sibling(h, z, beside)

    def own_finish(h):
        got(blocks(len(across)), gd.at[h, z])
        sibling(h, z, across)

    def far(step):
        return step // (nC - 1), near(lax.rem(step, nC - 1) + 1)

    def spread(step):
        h, k = far(step)
        own = slot(h, k, b, a)
        got(own, gz.at[h, k])
        for j in As:
            put(own, own, 0, g1.at[h, k], at(a_=j))
        for j in Bs:
            put(own, own, 0, g1.at[h, k], at(b_=j))
        put(own, own, 0, gs.at[h, k], sib)

    def forward(step):
        h, k = far(step)
        got(blocks(len(beside)), g1.at[h, k])
        diagonal(h, k)
        sibling(h, k, beside)

    def finish(step):
        h, k = far(step)
        got(blocks(len(across)), gd.at[h, k])
        sibling(h, k, across)

    def product(h, k):
        got(blocks(nA * nB), gs.at[h, k])
        for b_ in range(nB):
            tt = k * nB + b_
            lhs = flat_rows(H[pl.ds((h * nT + tt) * nP, nP)])
            acc[h] += jnp.dot(lhs, W[tt], preferred_element_type=f32)

    def multiply(step):
        product(*far(step))

    def own_multiply(h):
        hcopies[h].wait()
        product(h, z)

    tokens, width = acc.shape[1:]
    padded = stb.shape[-1]
    device_block = p * lax.axis_size("tensor") + t
    def of_chunk(column, h):
        return column.reshape(nP, nH, chunk, 1)[:, h].reshape(nP * chunk, 1)

    def hits(h):
        columns = device_block * width + lax.broadcasted_iota(jnp.int32, (tokens, width), 1)
        return of_chunk(target_col, h) == columns

    def stats_local(h):
        logits = acc[h]
        peak = jnp.max(logits, axis=1, keepdims=True)
        total = jnp.sum(jnp.exp(logits - peak), axis=1, keepdims=True)
        chosen = jnp.sum(jnp.where(hits(h), logits, 0.0), axis=1, keepdims=True)
        lane = lax.broadcasted_iota(jnp.int32, (tokens, 128), 1)
        packed = jnp.where(
            lane == 0, peak, jnp.where(lane == 1, total, jnp.where(lane == 2, chosen, 0.0))
        )
        if padded > tokens:
            packed = jnp.concatenate([packed, jnp.zeros((padded - tokens, 128), f32)], axis=0)
        stb[h] = jnp.transpose(packed)[0:8]
        for dev in Everyone:
            put(stb.at[h, pl.ds(0, 4)], st.at[h, device_block], 5, ssem.at[h], dev)
        st[h, device_block] = stb[h, 0:4]

    def stats_line(h):
        got(st.at[h, pl.ds(0, len(Everyone))], ssem.at[h])
        peaks, totals, chosen = (st[h, :, n : n + 1].reshape(len(Everyone) + 1, padded) for n in range(3))
        peak = jnp.max(peaks, axis=0, keepdims=True)
        total = jnp.sum(totals * jnp.exp(peaks - peak), axis=0, keepdims=True)
        picked = jnp.sum(chosen, axis=0, keepdims=True)
        log_total = peak + jnp.log(total)
        loss = jnp.broadcast_to(log_total - picked, (8, padded))
        lossb[h] = pltpu.roll(loss, lax.rem((h - p) * chunk + nP * padded, padded), axis=1)
        softmax = jnp.exp(acc[h] - to_column(log_total)[:tokens])
        dl[h] = (of_chunk(scale_col, h) * (softmax - hits(h).astype(f32))).astype(bf16)

    def order(step):
        return step // nC, near(nC - 1 - lax.rem(step, nC))

    def produce(step):
        h, k = order(step)
        for b_ in range(nB):
            tt = k * nB + b_
            for part in (pl.ds(0, cols // 2), pl.ds(cols // 2, cols // 2)):
                term = jnp.dot(dl[h], WT[tt, :, part], preferred_element_type=f32)
                Pb[h, tt, :, :, :, part] = term.reshape(nA, 2, chunk, cols // 2)
            put(Pb.at[h, tt, :, 1 - c], Sib.at[h, tt], 1, gs.at[h, k], sib)

    def stage1(step):
        h, k = order(step)
        got(Sib.at[h, pl.ds(0, nB)], gs.at[h, k])
        for b_ in range(nB):
            for a_ in range(nA):
                Sib[h, k * nB + b_, a_] = Sib[h, k * nB + b_, a_] + Pb[h, k * nB + b_, a_, c]
        for o in range(1, nA):
            at_, to = (o - 1) * nB, (nA - o - 1) * nB
            for b_ in range(nB):
                b1[h, k, at_ + b_] = Sib[h, k * nB + b_, As[o - 1], :, lo].astype(bf16)
            put(
                b1.at[h, k, pl.ds(at_, nB)], r1.at[h, k, pl.ds(to, nB)],
                2, g1.at[h, k], at(a_=As[o - 1]),
            )
        for o in range(1, nB):
            at_, to = base + (o - 1) * nA, base + (nB - o - 1) * nA
            for a_ in range(nA):
                b1[h, k, at_ + a_] = Sib[h, k * nB + Bs[o - 1], a_, :, hi].astype(bf16)
            put(
                b1.at[h, k, pl.ds(at_, nA)], r1.at[h, k, pl.ds(to, nA)],
                2, g1.at[h, k], at(b_=Bs[o - 1]),
            )

    base, turned = (nA - 1) * nB, nB - 1

    def from_x(h, k, j):
        return sum(r1[h, k, m * nB + j].astype(f32) for m in range(nA - 1))

    def from_y(h, k, j):
        return sum(r1[h, k, base + m * nA + j].astype(f32) for m in range(nB - 1))

    def stage2(step):
        h, k = order(step)
        tb = k * nB + b
        got(r1.at[h, k], g1.at[h, k])
        for o in range(1, nB):
            j = Bs[o - 1]
            b2[h, k, o - 1] = (Sib[h, k * nB + j, a, :, lo] + from_x(h, k, j)).astype(bf16)
            put(b2.at[h, k, o - 1], r2.at[h, k, nB - o - 1], 3, gd.at[h, k], at(b_=j))
        for o in range(1, nA):
            j = As[o - 1]
            b2[h, k, turned + o - 1] = (Sib[h, tb, j, :, hi] + from_y(h, k, j)).astype(bf16)
            put(
                b2.at[h, k, turned + o - 1], r2.at[h, k, turned + nA - o - 1],
                3, gd.at[h, k], at(a_=j),
            )
        Sib[h, tb, a, :, lo] = Sib[h, tb, a, :, lo] + from_x(h, k, b)
        Sib[h, tb, a, :, hi] = Sib[h, tb, a, :, hi] + from_y(h, k, a)

    def stage3(step):
        h, k = order(step)
        tb = k * nB + b
        got(r2.at[h, k], gd.at[h, k])
        low = Sib[h, tb, a, :, lo] + sum(r2[h, k, m].astype(f32) for m in range(turned))
        high = Sib[h, tb, a, :, hi] + sum(
            r2[h, k, turned + m].astype(f32) for m in range(nA - 1)
        )

        @pl.when(k != z)
        def _():
            zb[h, k, :, lo] = low.astype(bf16)
            zb[h, k, :, hi] = high.astype(bf16)
            put(zb.at[h, k], zr.at[h, z], 4, rz.at[h], at(z_=k))

        @pl.when(k == z)
        def _():
            keep[h, :, lo] = low
            keep[h, :, hi] = high

    def complete(h):
        got(zr.at[h, pl.ds(0, nC - 1)], rz.at[h])
        keep[h] = keep[h] + sum(zr[h, k].astype(f32) for k in Zs)
        pltpu.make_async_copy(keep.at[h], grad_out.at[pl.ds(h * chunk, chunk)], osem.at[h]).start()

    nF, nS = nH * (nC - 1), nH * nC
    B = 1 if nH > 1 else 0
    o2 = 2
    c0 = B + nC - 2 + 2 + 2 + 0
    begin = c0 + 2
    comm, work, stats, back = [], [], [], []
    add = lambda to, when, action, *args: to.append((when, None, action, args))
    own = lambda h: h if h < 2 else o2 + (h - 2) * nC
    for h in range(2, nH):
        if not False:
            add(comm, own(h) - 2, own_plane, h)
    for h in range(nH):
        add(comm, own(h), own_forward, h)
    for h in range(1, nH):
        add(comm, 1 + (h - 1) * 4, own_line, h, 0)
    comm.append((B, nF, spread, ()))
    comm.append((B + 2, nF, forward, ()))
    for h in range(nH):
        add(comm, own(h) + 2, own_finish, h)
    comm.append((B + 2 + 2, nF, finish, ()))
    for h in range(nH):
        add(work, own(h) + 2 + 1, own_multiply, h)
    work.append((B + 2 + 2 + 0, nF, multiply, ()))
    turning = [(1, nT, turn, ())]
    add(comm, 0, wcopy.wait)
    for h in range(nH):
        w = c0 + h * (nC - 1)
        add(stats, w + 2 + (h * 2) // 2, stats_line, h)
        add(work, w, stats_local, h)
    back += [(begin + 1, nS, stage1, ()), (begin + 1 + 2, nS, stage2, ()), (begin + 1 + 2 + 2, nS, stage3, ()), (begin, nS, produce, ())]
    end = 1 + 2 + 2
    for h in range(nH):
        add(back, begin + (h + 1) * nC - 1 + end + (2 if h < nH - 1 else 0), complete, h)
    plans = [comm, turning, stats, back, work]
    length = begin + nS + end

    with jax.named_scope("barrier"):
        pl.semaphore_wait(barrier, len(peers))
    own_plane(0)
    own_line(0, 1)
    for copy in [tcopy, kcopy] + hcopies + [wcopy]:
        copy.start()
    with jax.named_scope("zero"):
        acc[...] = jnp.zeros_like(acc)
        tcopy.wait()
        kcopy.wait()
        target_col = to_column(tbuf[...].reshape(1, -1).astype(f32)).astype(jnp.int32)
        scale_col = loss_scale * to_column(wbuf[...].reshape(1, -1))
    own_line(0, 2)
    if nH > 1:
        own_plane(1)

    def during(i, begin, count, action):
        @pl.when((i >= begin) & (i < begin + count))
        def _():
            with jax.named_scope(action.__name__):
                action(i - begin)

    def once(i, when, action, *args):
        @pl.when(i == when)
        def _():
            with jax.named_scope(action.__name__):
                action(*args)

    def step(i, carry):
        for entries in plans:
            first_i = min(e[0] for e in entries)
            last_i = max(e[0] + (e[1] or 1) for e in entries)

            @pl.when((i >= first_i) & (i < last_i))
            def _():
                for when, count, action, args in entries:
                    if count is None:
                        once(i, when, action, *args)
                    else:
                        during(i, when, count, action)
        return carry

    lax.fori_loop(0, length, step, 0)
    with jax.named_scope("loss"):
        lane = lax.broadcasted_iota(jnp.int32, (8, padded), 1)
        loss = lossb[0]
        for h in range(1, nH):
            loss = jnp.where(lane >= h * chunk, lossb[h], loss)
        lossrow[...] = loss[0, :rows]
        lcopy = pltpu.make_async_copy(lossrow, loss_out, lsem.at[1])
        lcopy.start()

    with jax.named_scope('drain'):
        sent(blocks(nH * (nT * nP - 1)), 0)
        sent(Sib, 1)
        sent(b1, 2)
        sent(b2, 3)
        sent(zb.at[:, pl.ds(0, nC - 1)], 4)
        sent(st.at[:, pl.ds(0, len(Everyone))], 5)
        for h in range(nH):
            pltpu.make_async_copy(keep.at[h], grad_out.at[pl.ds(h * chunk, chunk)], osem.at[h]).wait()
        lcopy.wait()


def hand_over(loss, grad, loss_out, grad_out):
    loss_out[...] = loss[...]
    grad_out[...] = grad[...]


def local(hidden, weight, targets, token_weight):
    rows, cols = hidden.shape
    n_pipe, n_tensor = lax.axis_size("pipe"), lax.axis_size("tensor")
    nA, nB, nC = n_pipe // 2, 2, n_tensor // 2
    tokens, width = targets.shape[0], weight.shape[1]
    vmem, dma = pltpu.VMEM, pltpu.SemaphoreType.DMA
    nH = 3 if rows % (16 * 3) == 0 else 1
    chunk = rows // nH
    half = cols // 2
    n1, n2 = (nA - 1) * nB + (nB - 1) * nA, nB + nA - 2
    part = n_pipe * chunk
    padded = -(-part // 128) * 128
    token_loss, hidden_grad = pl.pallas_call(
        functools.partial(kernel, nA, nB, nC, nH),
        out_shape=(
            jax.ShapeDtypeStruct((rows,), f32),
            jax.ShapeDtypeStruct((rows, cols), f32),
        ),
        in_specs=[pl.BlockSpec(memory_space=pl.ANY)] * 4,
        out_specs=[pl.BlockSpec(memory_space=pl.ANY)] * 2,
        scratch_shapes=[
            vmem((nH * n_tensor * n_pipe, chunk, cols), bf16),
            vmem((n_tensor, cols, width), bf16),
            vmem((n_tensor, width, cols), bf16),
            vmem((nH, part, width), f32),
            vmem((nH, part, width), bf16),
            vmem((nH, n_tensor, nA, 2, chunk, cols), f32),
            vmem((nH, n_tensor, nA, chunk, cols), f32),
            vmem((nH, nC, n1, chunk, half), bf16),
            vmem((nH, nC, n1, chunk, half), bf16),
            vmem((nH, nC, n2, chunk, half), bf16),
            vmem((nH, nC, n2, chunk, half), bf16),
            vmem((nH, nC, chunk, cols), bf16),
            vmem((nH, nC, chunk, cols), bf16),
            vmem((nH, chunk, cols), f32),
            vmem((nH, 8, padded), f32),
            vmem((nH, n_pipe * n_tensor, 4, padded), f32),
            vmem((nH, 8, padded), f32),
            vmem((rows,), f32),
            vmem((tokens,), jnp.int32),
            vmem((tokens,), f32),
            dma((3,)),
            dma((nH,)),
            dma((nH,)),
            dma((6,)),
            dma((nH, nC)),
            dma((nH, nC)),
            dma((nH, nC)),
            dma((nH, nC)),
            dma((nH,)),
            dma((nH,)),
        ],
        compiler_params=pltpu.CompilerParams(
            collective_id=0, has_side_effects=True, vmem_limit_bytes=52 * 1024 * 1024
        ),
    )(
        pltpu.with_memory_space_constraint(hidden, pltpu.HBM),
        weight.reshape(n_tensor, cols, width),
        pltpu.with_memory_space_constraint(targets, pltpu.HBM),
        pltpu.with_memory_space_constraint(token_weight, pltpu.HBM),
    )
    return pl.pallas_call(
        hand_over,
        out_shape=(
            jax.ShapeDtypeStruct((rows,), f32),
            jax.ShapeDtypeStruct((rows, cols), f32),
        ),
        in_specs=[pl.BlockSpec(memory_space=vmem)] * 2,
        out_specs=[pl.BlockSpec(memory_space=vmem)] * 2,

        compiler_params=pltpu.CompilerParams(vmem_limit_bytes=4 * 1024 * 1024),
    )(token_loss, hidden_grad)


def solution(mesh):
    in_specs = (P("pipe", "tensor"), P(None, ("pipe", "tensor")), P(), P())
    out_specs = (P("pipe"), P("pipe", "tensor"))
    return jax.shard_map(local, mesh=mesh, in_specs=in_specs, out_specs=out_specs, check_vma=False)
```

```python
import functools

import jax
import jax.numpy as jnp
from jax import lax
from jax.experimental import pallas as pl
from jax.experimental.pallas import tpu as pltpu
from jax.sharding import PartitionSpec as P

loss_scale = 32.0
f32, bf16 = jnp.float32, jnp.bfloat16
MESH = pl.DeviceIdType.MESH


def flat_rows(block):
    n, rows, width = block.shape
    if rows % 16:
        return block.astype(f32).reshape(n * rows, width).astype(bf16)
    return block.reshape(n * rows, width)


def to_column(row):
    return jnp.transpose(jnp.broadcast_to(row, (128, row.shape[1])))[:, :1]


def kernel(
    nA, nB, nC, nH,
    hidden, weight, targets, token_weight,
    loss_out, grad_out,
    H, W, WT, acc, dl, Pb, Sib, b1, r1, b2, r2, zb, zr, keep, stb, st, lossb, lossrow, tbuf, wbuf,
    lsem, hsem, osem, sends, g1, gd, gs, gz, rz, ssem,
):
    rows, cols = hidden.shape
    chunk = rows // nH
    half = cols // 2
    nP, nT = nA * 2, nB * nC
    lo, hi = pl.ds(0, half), pl.ds(half, half)
    p, t = lax.axis_index("pipe"), lax.axis_index("tensor")
    a, c = p // 2, lax.rem(p, 2)
    b, z = lax.rem(t, nB), t // nB

    def at(a_=None, b_=None, z_=None, c_=None):
        a_, b_ = (a if a_ is None else a_), (b if b_ is None else b_)
        z_, c_ = (z if z_ is None else z_), (c if c_ is None else c_)
        return {"pipe": a_ * 2 + c_, "tensor": z_ * nB + b_}

    left, right = z, nC - 1 - z
    both = jnp.minimum(left, right)
    longer = jnp.where(left > right, -1, 1)

    def near(i):
        d = (i + 1) // 2
        turn = jnp.where(lax.rem(i, 2) == 1, -d, d)
        return z + jnp.where(i <= 2 * both, turn, longer * (i - both))

    As = [lax.rem(a + o, nA) for o in range(1, nA)]
    Bs = [lax.rem(b + o, nB) for o in range(1, nB)]
    Zs = [near(jnp.int32(i)) for i in range(1, nC)]
    sib = at(c_=1 - c)
    Everyone = [
        at(a_=a_, b_=b_, c_=c_, z_=z_)
        for z_ in [z] + Zs for a_ in [a] + As for b_ in [b] + Bs for c_ in (c, 1 - c)
    ][1:]
    peers = Everyone[: nP * nB - 1] + [at(z_=k) for k in Zs]

    def put(src, dst, send, recv, dev):
        pltpu.make_async_remote_copy(
            src_ref=src, dst_ref=dst, send_sem=sends.at[send], recv_sem=recv,
            device_id=dev, device_id_type=MESH,
        ).start()

    def got(dst, recv):
        pltpu.make_async_remote_copy(
            src_ref=dst, dst_ref=dst, send_sem=sends.at[0], recv_sem=recv,
            device_id=sib, device_id_type=MESH,
        ).wait_recv()

    def sent(src, send):
        pltpu.make_async_remote_copy(
            src_ref=src, dst_ref=src, send_sem=sends.at[send], recv_sem=rz.at[0],
            device_id=sib, device_id_type=MESH,
        ).wait_send()

    barrier = pltpu.get_barrier_semaphore()
    for dev in peers:
        pl.semaphore_signal(barrier, inc=1, device_id=dev, device_id_type=MESH)

    def where(h, k, b_, a_, c_=None):
        return (h * nT + k * nB + b_) * nP + a_ * 2 + (c if c_ is None else c_)

    def slot(h, k, b_, a_):
        return H.at[where(h, k, b_, a_)]

    def blocks(n):
        return H.at[pl.ds(0, n)]

    hcopies = [
        pltpu.make_async_copy(
            hidden.at[pl.ds(h * chunk, chunk)], slot(h, z, b, a), hsem.at[h]
        )
        for h in range(nH)
    ]
    tcopy = pltpu.make_async_copy(targets, tbuf, lsem.at[1])
    kcopy = pltpu.make_async_copy(token_weight, wbuf, lsem.at[2])
    wcopy = pltpu.make_async_copy(weight, W, lsem.at[0])

    def own_plane(h):
        src, own = hidden.at[pl.ds(h * chunk, chunk)], slot(h, z, b, a)
        for j in As:
            put(src, own, 0, g1.at[h, z], at(a_=j))
        for j in Bs:
            put(src, own, 0, g1.at[h, z], at(b_=j))
        put(src, own, 0, gs.at[h, z], sib)

    def own_line(h, group):
        src, own = hidden.at[pl.ds(h * chunk, chunk)], slot(h, z, b, a)
        for k in (Zs, Zs[:2], Zs[2:])[group]:
            put(src, own, 0, gz.at[h, z], at(z_=k))

    def turn(n):
        WT[n] = jnp.transpose(W[n])

    def turns(first_, last_):
        for n in range(first_, last_):
            turn(n)

    def diagonal(h, k):
        for j in As:
            for m in Bs:
                ref = slot(h, k, b, j).at[:, lo]
                put(ref, ref, 0, gd.at[h, k], at(b_=m))
        for j in Bs:
            for m in As:
                ref = slot(h, k, j, a).at[:, hi]
                put(ref, ref, 0, gd.at[h, k], at(a_=m))

    def sibling(h, k, places):
        for b_, a_ in places:
            put(slot(h, k, b_, a_), slot(h, k, b_, a_), 0, gs.at[h, k], sib)

    beside = [(b, j) for j in As] + [(j, a) for j in Bs]
    across = [(m, j) for j in As for m in Bs]

    def own_forward(h):
        got(blocks(len(beside)), g1.at[h, z])
        diagonal(h, z)
        sibling(h, z, beside)

    def own_finish(h):
        got(blocks(len(across)), gd.at[h, z])
        sibling(h, z, across)

    def far(step):
        return step // (nC - 1), near(lax.rem(step, nC - 1) + 1)

    def spread(step):
        h, k = far(step)
        own = slot(h, k, b, a)
        got(own, gz.at[h, k])
        for j in As:
            put(own, own, 0, g1.at[h, k], at(a_=j))
        for j in Bs:
            put(own, own, 0, g1.at[h, k], at(b_=j))
        put(own, own, 0, gs.at[h, k], sib)

    def forward(step):
        h, k = far(step)
        got(blocks(len(beside)), g1.at[h, k])
        diagonal(h, k)
        sibling(h, k, beside)

    def finish(step):
        h, k = far(step)
        got(blocks(len(across)), gd.at[h, k])
        sibling(h, k, across)

    def product(h, k):
        got(blocks(nA * nB), gs.at[h, k])
        for b_ in range(nB):
            tt = k * nB + b_
            lhs = flat_rows(H[pl.ds((h * nT + tt) * nP, nP)])
            acc[h] += jnp.dot(lhs, W[tt], preferred_element_type=f32)

    def multiply(step):
        product(*far(step))

    def own_multiply(h):
        hcopies[h].wait()
        product(h, z)

    tokens, width = acc.shape[1:]
    padded = stb.shape[-1]
    device_block = p * lax.axis_size("tensor") + t
    def of_chunk(column, h):
        return column.reshape(nP, nH, chunk, 1)[:, h].reshape(nP * chunk, 1)

    def hits(h):
        columns = device_block * width + lax.broadcasted_iota(jnp.int32, (tokens, width), 1)
        return of_chunk(target_col, h) == columns

    def stats_local(h):
        logits = acc[h]
        peak = jnp.max(logits, axis=1, keepdims=True)
        total = jnp.sum(jnp.exp(logits - peak), axis=1, keepdims=True)
        chosen = jnp.sum(jnp.where(hits(h), logits, 0.0), axis=1, keepdims=True)
        lane = lax.broadcasted_iota(jnp.int32, (tokens, 128), 1)
        packed = jnp.where(
            lane == 0, peak, jnp.where(lane == 1, total, jnp.where(lane == 2, chosen, 0.0))
        )
        if padded > tokens:
            packed = jnp.concatenate([packed, jnp.zeros((padded - tokens, 128), f32)], axis=0)
        stb[h] = jnp.transpose(packed)[0:8]
        for dev in Everyone:
            put(stb.at[h, pl.ds(0, 4)], st.at[h, device_block], 5, ssem.at[h], dev)
        st[h, device_block] = stb[h, 0:4]

    def stats_line(h):
        got(st.at[h, pl.ds(0, len(Everyone))], ssem.at[h])
        peaks, totals, chosen = (st[h, :, n : n + 1].reshape(len(Everyone) + 1, padded) for n in range(3))
        peak = jnp.max(peaks, axis=0, keepdims=True)
        total = jnp.sum(totals * jnp.exp(peaks - peak), axis=0, keepdims=True)
        picked = jnp.sum(chosen, axis=0, keepdims=True)
        log_total = peak + jnp.log(total)
        loss = jnp.broadcast_to(log_total - picked, (8, padded))
        lossb[h] = pltpu.roll(loss, lax.rem((h - p) * chunk + nP * padded, padded), axis=1)
        softmax = jnp.exp(acc[h] - to_column(log_total)[:tokens])
        dl[h] = (of_chunk(scale_col, h) * (softmax - hits(h).astype(f32))).astype(bf16)

    def pick(step, values):
        out = jnp.int32(values[0])
        for n in range(1, len(values)):
            if values[n] != values[n - 1]:
                out = out + jnp.where(step >= n, values[n] - values[n - 1], 0)
        return out

    def order(step):
        return pick(step, [h for h, _ in turns_]), near(pick(step, [i for _, i in turns_]))

    def produce(step):
        h, k = order(step)
        for b_ in range(nB):
            tt = k * nB + b_
            for part in (pl.ds(0, cols // 2), pl.ds(cols // 2, cols // 2)):
                term = jnp.dot(dl[h], WT[tt, :, part], preferred_element_type=f32)
                Pb[h, tt, :, :, :, part] = term.reshape(nA, 2, chunk, cols // 2)
            put(Pb.at[h, tt, :, 1 - c], Sib.at[h, tt], 1, gs.at[h, k], sib)

    def stage1(step):
        h, k = order(step)
        got(Sib.at[h, pl.ds(0, nB)], gs.at[h, k])
        for b_ in range(nB):
            for a_ in range(nA):
                Sib[h, k * nB + b_, a_] = Sib[h, k * nB + b_, a_] + Pb[h, k * nB + b_, a_, c]
        for o in range(1, nA):
            at_, to = (o - 1) * nB, (nA - o - 1) * nB
            for b_ in range(nB):
                b1[h, k, at_ + b_] = Sib[h, k * nB + b_, As[o - 1], :, lo].astype(bf16)
            put(
                b1.at[h, k, pl.ds(at_, nB)], r1.at[h, k, pl.ds(to, nB)],
                2, g1.at[h, k], at(a_=As[o - 1]),
            )
        for o in range(1, nB):
            at_, to = base + (o - 1) * nA, base + (nB - o - 1) * nA
            for a_ in range(nA):
                b1[h, k, at_ + a_] = Sib[h, k * nB + Bs[o - 1], a_, :, hi].astype(bf16)
            put(
                b1.at[h, k, pl.ds(at_, nA)], r1.at[h, k, pl.ds(to, nA)],
                2, g1.at[h, k], at(b_=Bs[o - 1]),
            )

    base, turned = (nA - 1) * nB, nB - 1

    def from_x(h, k, j):
        return sum(r1[h, k, m * nB + j].astype(f32) for m in range(nA - 1))

    def from_y(h, k, j):
        return sum(r1[h, k, base + m * nA + j].astype(f32) for m in range(nB - 1))

    def stage2(step):
        h, k = order(step)
        tb = k * nB + b
        got(r1.at[h, k], g1.at[h, k])
        for o in range(1, nB):
            j = Bs[o - 1]
            b2[h, k, o - 1] = (Sib[h, k * nB + j, a, :, lo] + from_x(h, k, j)).astype(bf16)
            put(b2.at[h, k, o - 1], r2.at[h, k, nB - o - 1], 3, gd.at[h, k], at(b_=j))
        for o in range(1, nA):
            j = As[o - 1]
            b2[h, k, turned + o - 1] = (Sib[h, tb, j, :, hi] + from_y(h, k, j)).astype(bf16)
            put(
                b2.at[h, k, turned + o - 1], r2.at[h, k, turned + nA - o - 1],
                3, gd.at[h, k], at(a_=j),
            )
        Sib[h, tb, a, :, lo] = Sib[h, tb, a, :, lo] + from_x(h, k, b)
        Sib[h, tb, a, :, hi] = Sib[h, tb, a, :, hi] + from_y(h, k, a)

    def stage3(step):
        h, k = order(step)
        tb = k * nB + b
        got(r2.at[h, k], gd.at[h, k])
        low = Sib[h, tb, a, :, lo] + sum(r2[h, k, m].astype(f32) for m in range(turned))
        high = Sib[h, tb, a, :, hi] + sum(
            r2[h, k, turned + m].astype(f32) for m in range(nA - 1)
        )

        @pl.when(k != z)
        def _():
            zb[h, k, :, lo] = low.astype(bf16)
            zb[h, k, :, hi] = high.astype(bf16)
            put(zb.at[h, k], zr.at[h, z], 4, rz.at[h], at(z_=k))

        @pl.when(k == z)
        def _():
            keep[h, :, lo] = low
            keep[h, :, hi] = high

    def complete(h):
        got(zr.at[h, pl.ds(0, nC - 1)], rz.at[h])
        keep[h] = keep[h] + sum(zr[h, k].astype(f32) for k in Zs)
        pltpu.make_async_copy(keep.at[h], grad_out.at[pl.ds(h * chunk, chunk)], osem.at[h]).start()

    nF, nS = nH * (nC - 1), nH * nC
    turns_ = [(h, nC - 1 - i) for h in range(nH) for i in range(nC)]
    later = list(range(nH))
    if nH == 3 and nC == 4:
        turns_ = [(0, i) for i in (3, 2, 1, 0)] + [(1, i) for i in (3, 2, 1)]
        turns_ += [(2, i) for i in (3, 2, 1)] + [(1, 0), (2, 0)]
        later = (0, 1, 1)
    B = 2 if nH > 1 else 0
    o2 = 2
    c0 = B + nC - 2 + 2 + 2 + 0
    begin = c0 + 2 + 0
    comm, work, stats, back = [], [], [], []
    add = lambda to, when, action, *args: to.append((when, None, action, args))
    own = lambda h: h if h < 2 else o2 + (h - 2) * nC
    for h in range(2, nH):
        if not False:
            add(comm, own(h) - 2, own_plane, h)
    for h in range(nH):
        add(comm, own(h), own_forward, h)
    for h in range(1, nH):
        add(comm, 2 + (h - 1) * 4, own_line, h, 0)
    comm.append((B, nF, spread, ()))
    comm.append((B + 2, nF, forward, ()))
    for h in range(nH):
        add(comm, own(h) + 2, own_finish, h)
    comm.append((B + 2 + 2, nF, finish, ()))
    for h in range(nH):
        add(work, own(h) + 2 + 1, own_multiply, h)
    work.append((B + 2 + 2 + 0, nF, multiply, ()))
    turning = [(1, nT, turn, ())]
    add(comm, 0, wcopy.wait)
    for h in range(nH):
        w = c0 + h * (nC - 1)
        add(stats, w + 2 + later[h], stats_line, h)
        add(work, w, stats_local, h)
    back += [(begin + 1, nS, stage1, ()), (begin + 1 + 2, nS, stage2, ()), (begin + 1 + 2 + 2, nS, stage3, ()), (begin, nS, produce, ())]
    end = 1 + 2 + 2
    for h in range(nH):
        at_ = turns_.index((h, 0)) + (2 if h < nH - 1 else 0)
        add(back, begin + min(at_, nS - 1) + end, complete, h)
    plans = [comm, turning, stats, back, work]
    length = begin + nS + end

    with jax.named_scope("barrier"):
        pl.semaphore_wait(barrier, len(peers))
    own_plane(0)
    own_line(0, 1)
    for copy in [tcopy, kcopy] + hcopies + [wcopy]:
        copy.start()
    with jax.named_scope("zero"):
        acc[...] = jnp.zeros_like(acc)
        tcopy.wait()
        kcopy.wait()
        target_col = to_column(tbuf[...].reshape(1, -1).astype(f32)).astype(jnp.int32)
        scale_col = loss_scale * to_column(wbuf[...].reshape(1, -1))
    own_line(0, 2)
    if nH > 1:
        own_plane(1)

    def during(i, begin, count, action):
        @pl.when((i >= begin) & (i < begin + count))
        def _():
            with jax.named_scope(action.__name__):
                action(i - begin)

    def once(i, when, action, *args):
        @pl.when(i == when)
        def _():
            with jax.named_scope(action.__name__):
                action(*args)

    def step(i, carry):
        for entries in plans:
            first_i = min(e[0] for e in entries)
            last_i = max(e[0] + (e[1] or 1) for e in entries)

            @pl.when((i >= first_i) & (i < last_i))
            def _():
                for when, count, action, args in entries:
                    if count is None:
                        once(i, when, action, *args)
                    else:
                        during(i, when, count, action)
        return carry

    lax.fori_loop(0, length, step, 0)
    with jax.named_scope("loss"):
        lane = lax.broadcasted_iota(jnp.int32, (8, padded), 1)
        loss = lossb[0]
        for h in range(1, nH):
            loss = jnp.where(lane >= h * chunk, lossb[h], loss)
        lossrow[...] = loss[0, :rows]
        lcopy = pltpu.make_async_copy(lossrow, loss_out, lsem.at[1])
        lcopy.start()

    with jax.named_scope('drain'):
        sent(blocks(nH * (nT * nP - 1)), 0)
        sent(Sib, 1)
        sent(b1, 2)
        sent(b2, 3)
        sent(zb.at[:, pl.ds(0, nC - 1)], 4)
        sent(st.at[:, pl.ds(0, len(Everyone))], 5)
        for h in range(nH):
            pltpu.make_async_copy(keep.at[h], grad_out.at[pl.ds(h * chunk, chunk)], osem.at[h]).wait()
        lcopy.wait()


def hand_over(loss, grad, loss_out, grad_out):
    loss_out[...] = loss[...]
    grad_out[...] = grad[...]


def local(hidden, weight, targets, token_weight):
    rows, cols = hidden.shape
    n_pipe, n_tensor = lax.axis_size("pipe"), lax.axis_size("tensor")
    nA, nB, nC = n_pipe // 2, 2, n_tensor // 2
    tokens, width = targets.shape[0], weight.shape[1]
    vmem, dma = pltpu.VMEM, pltpu.SemaphoreType.DMA
    nH = 3 if rows % (16 * 3) == 0 else 1
    chunk = rows // nH
    half = cols // 2
    n1, n2 = (nA - 1) * nB + (nB - 1) * nA, nB + nA - 2
    part = n_pipe * chunk
    padded = -(-part // 128) * 128
    token_loss, hidden_grad = pl.pallas_call(
        functools.partial(kernel, nA, nB, nC, nH),
        out_shape=(
            jax.ShapeDtypeStruct((rows,), f32),
            jax.ShapeDtypeStruct((rows, cols), f32),
        ),
        in_specs=[pl.BlockSpec(memory_space=pl.ANY)] * 4,
        out_specs=[pl.BlockSpec(memory_space=pl.ANY)] * 2,
        scratch_shapes=[
            vmem((nH * n_tensor * n_pipe, chunk, cols), bf16),
            vmem((n_tensor, cols, width), bf16),
            vmem((n_tensor, width, cols), bf16),
            vmem((nH, part, width), f32),
            vmem((nH, part, width), bf16),
            vmem((nH, n_tensor, nA, 2, chunk, cols), f32),
            vmem((nH, n_tensor, nA, chunk, cols), f32),
            vmem((nH, nC, n1, chunk, half), bf16),
            vmem((nH, nC, n1, chunk, half), bf16),
            vmem((nH, nC, n2, chunk, half), bf16),
            vmem((nH, nC, n2, chunk, half), bf16),
            vmem((nH, nC, chunk, cols), bf16),
            vmem((nH, nC, chunk, cols), bf16),
            vmem((nH, chunk, cols), f32),
            vmem((nH, 8, padded), f32),
            vmem((nH, n_pipe * n_tensor, 4, padded), f32),
            vmem((nH, 8, padded), f32),
            vmem((rows,), f32),
            vmem((tokens,), jnp.int32),
            vmem((tokens,), f32),
            dma((3,)),
            dma((nH,)),
            dma((nH,)),
            dma((6,)),
            dma((nH, nC)),
            dma((nH, nC)),
            dma((nH, nC)),
            dma((nH, nC)),
            dma((nH,)),
            dma((nH,)),
        ],
        compiler_params=pltpu.CompilerParams(
            collective_id=0, has_side_effects=True, vmem_limit_bytes=52 * 1024 * 1024
        ),
    )(
        pltpu.with_memory_space_constraint(hidden, pltpu.HBM),
        weight.reshape(n_tensor, cols, width),
        pltpu.with_memory_space_constraint(targets, pltpu.HBM),
        pltpu.with_memory_space_constraint(token_weight, pltpu.HBM),
    )
    return pl.pallas_call(
        hand_over,
        out_shape=(
            jax.ShapeDtypeStruct((rows,), f32),
            jax.ShapeDtypeStruct((rows, cols), f32),
        ),
        in_specs=[pl.BlockSpec(memory_space=vmem)] * 2,
        out_specs=[pl.BlockSpec(memory_space=vmem)] * 2,

        compiler_params=pltpu.CompilerParams(vmem_limit_bytes=4 * 1024 * 1024),
    )(token_loss, hidden_grad)


def solution(mesh):
    in_specs = (P("pipe", "tensor"), P(None, ("pipe", "tensor")), P(), P())
    out_specs = (P("pipe"), P("pipe", "tensor"))
    return jax.shard_map(local, mesh=mesh, in_specs=in_specs, out_specs=out_specs, check_vma=False)
```

```python
import functools

import jax
import jax.numpy as jnp
from jax import lax
from jax.experimental import pallas as pl
from jax.experimental.pallas import tpu as pltpu
from jax.sharding import PartitionSpec as P

loss_scale = 32.0
f32, bf16 = jnp.float32, jnp.bfloat16
MESH = pl.DeviceIdType.MESH


def flat_rows(block):
    n, rows, width = block.shape
    if rows % 16:
        return block.astype(f32).reshape(n * rows, width).astype(bf16)
    return block.reshape(n * rows, width)


def to_column(row):
    return jnp.transpose(jnp.broadcast_to(row, (128, row.shape[1])))[:, :1]


def kernel(
    nA, nB, nC, nH,
    hidden, weight, targets, token_weight,
    loss_out, grad_out,
    H, W, WT, acc, dl, Pb, Sib, b1, r1, b2, r2, zb, zr, keep, stb, st, lossb, lossrow, tbuf, wbuf,
    lsem, hsem, osem, sends, g1, gd, gs, gz, rz, ssem,
):
    rows, cols = hidden.shape
    chunk = rows // nH
    half = cols // 2
    nP, nT = nA * 2, nB * nC
    lo, hi = pl.ds(0, half), pl.ds(half, half)
    p, t = lax.axis_index("pipe"), lax.axis_index("tensor")
    a, c = p // 2, lax.rem(p, 2)
    b, z = lax.rem(t, nB), t // nB

    def at(a_=None, b_=None, z_=None, c_=None):
        a_, b_ = (a if a_ is None else a_), (b if b_ is None else b_)
        z_, c_ = (z if z_ is None else z_), (c if c_ is None else c_)
        return {"pipe": a_ * 2 + c_, "tensor": z_ * nB + b_}

    left, right = z, nC - 1 - z
    both = jnp.minimum(left, right)
    longer = jnp.where(left > right, -1, 1)

    def near(i):
        d = (i + 1) // 2
        turn = jnp.where(lax.rem(i, 2) == 1, -d, d)
        return z + jnp.where(i <= 2 * both, turn, longer * (i - both))

    As = [lax.rem(a + o, nA) for o in range(1, nA)]
    Bs = [lax.rem(b + o, nB) for o in range(1, nB)]
    Zs = [near(jnp.int32(i)) for i in range(1, nC)]
    sib = at(c_=1 - c)
    Everyone = [
        at(a_=a_, b_=b_, c_=c_, z_=z_)
        for z_ in [z] + Zs for a_ in [a] + As for b_ in [b] + Bs for c_ in (c, 1 - c)
    ][1:]
    peers = Everyone[: nP * nB - 1] + [at(z_=k) for k in Zs]

    def put(src, dst, send, recv, dev):
        pltpu.make_async_remote_copy(
            src_ref=src, dst_ref=dst, send_sem=sends.at[send], recv_sem=recv,
            device_id=dev, device_id_type=MESH,
        ).start()

    def got(dst, recv):
        pltpu.make_async_remote_copy(
            src_ref=dst, dst_ref=dst, send_sem=sends.at[0], recv_sem=recv,
            device_id=sib, device_id_type=MESH,
        ).wait_recv()

    def sent(src, send):
        pltpu.make_async_remote_copy(
            src_ref=src, dst_ref=src, send_sem=sends.at[send], recv_sem=rz.at[0],
            device_id=sib, device_id_type=MESH,
        ).wait_send()

    barrier = pltpu.get_barrier_semaphore()
    for dev in peers:
        pl.semaphore_signal(barrier, inc=1, device_id=dev, device_id_type=MESH)

    def where(h, k, b_, a_, c_=None):
        return (h * nT + k * nB + b_) * nP + a_ * 2 + (c if c_ is None else c_)

    def slot(h, k, b_, a_):
        return H.at[where(h, k, b_, a_)]

    def blocks(n):
        return H.at[pl.ds(0, n)]

    hcopies = [
        pltpu.make_async_copy(
            hidden.at[pl.ds(h * chunk, chunk)], slot(h, z, b, a), hsem.at[h]
        )
        for h in range(nH)
    ]
    tcopy = pltpu.make_async_copy(targets, tbuf, lsem.at[1])
    kcopy = pltpu.make_async_copy(token_weight, wbuf, lsem.at[2])
    wcopy = pltpu.make_async_copy(weight, W, lsem.at[0])

    def own_plane(h):
        src, own = hidden.at[pl.ds(h * chunk, chunk)], slot(h, z, b, a)
        for j in As:
            put(src, own, 0, g1.at[h, z], at(a_=j))
        for j in Bs:
            put(src, own, 0, g1.at[h, z], at(b_=j))
        put(src, own, 0, gs.at[h, z], sib)

    def own_line(h, group):
        src, own = hidden.at[pl.ds(h * chunk, chunk)], slot(h, z, b, a)
        for k in (Zs, Zs[:2], Zs[2:])[group]:
            put(src, own, 0, gz.at[h, z], at(z_=k))

    def turn(n):
        for m in range(share):
            WT[n * share + m] = jnp.transpose(W[n * share + m])

    def diagonal(h, k):
        for j in As:
            for m in Bs:
                ref = slot(h, k, b, j).at[:, lo]
                put(ref, ref, 0, gd.at[h, k], at(b_=m))
        for j in Bs:
            for m in As:
                ref = slot(h, k, j, a).at[:, hi]
                put(ref, ref, 0, gd.at[h, k], at(a_=m))

    def sibling(h, k, places):
        for b_, a_ in places:
            put(slot(h, k, b_, a_), slot(h, k, b_, a_), 0, gs.at[h, k], sib)

    beside = [(b, j) for j in As] + [(j, a) for j in Bs]
    across = [(m, j) for j in As for m in Bs]

    def own_forward(h):
        got(blocks(len(beside)), g1.at[h, z])
        diagonal(h, z)
        sibling(h, z, beside)

    def own_finish(h):
        got(blocks(len(across)), gd.at[h, z])
        sibling(h, z, across)

    def far(step):
        return step // (nC - 1), near(lax.rem(step, nC - 1) + 1)

    def spread(step):
        h, k = far(step)
        own = slot(h, k, b, a)
        got(own, gz.at[h, k])
        for j in As:
            put(own, own, 0, g1.at[h, k], at(a_=j))
        for j in Bs:
            put(own, own, 0, g1.at[h, k], at(b_=j))
        put(own, own, 0, gs.at[h, k], sib)

    def forward(step):
        h, k = far(step)
        got(blocks(len(beside)), g1.at[h, k])
        diagonal(h, k)
        sibling(h, k, beside)

    def finish(step):
        h, k = far(step)
        got(blocks(len(across)), gd.at[h, k])
        sibling(h, k, across)

    def product(h, k):
        got(blocks(nA * nB), gs.at[h, k])
        for b_ in range(nB):
            tt = k * nB + b_
            lhs = flat_rows(H[pl.ds((h * nT + tt) * nP, nP)])
            acc[h] += jnp.dot(lhs, W[tt], preferred_element_type=f32)

    def multiply(step):
        product(*far(step))

    def own_multiply(h):
        hcopies[h].wait()
        product(h, z)

    tokens, width = acc.shape[1:]
    padded = stb.shape[-1]
    device_block = p * lax.axis_size("tensor") + t
    def of_chunk(column, h):
        return column.reshape(nP, nH, chunk, 1)[:, h].reshape(nP * chunk, 1)

    def hits(h):
        columns = device_block * width + lax.broadcasted_iota(jnp.int32, (tokens, width), 1)
        return of_chunk(target_col, h) == columns

    def stats_local(h):
        logits = acc[h]
        peak = jnp.max(logits, axis=1, keepdims=True)
        total = jnp.sum(jnp.exp(logits - peak), axis=1, keepdims=True)
        chosen = jnp.sum(jnp.where(hits(h), logits, 0.0), axis=1, keepdims=True)
        lane = lax.broadcasted_iota(jnp.int32, (tokens, 128), 1)
        packed = jnp.where(
            lane == 0, peak, jnp.where(lane == 1, total, jnp.where(lane == 2, chosen, 0.0))
        )
        if padded > tokens:
            packed = jnp.concatenate([packed, jnp.zeros((padded - tokens, 128), f32)], axis=0)
        stb[h] = jnp.transpose(packed)[0:8]
        for dev in Everyone:
            put(stb.at[h, pl.ds(0, 4)], st.at[h, device_block], 5, ssem.at[h], dev)
        st[h, device_block] = stb[h, 0:4]

    def stats_line(h):
        got(st.at[h, pl.ds(0, len(Everyone))], ssem.at[h])
        peaks, totals, chosen = (st[h, :, n : n + 1].reshape(len(Everyone) + 1, padded) for n in range(3))
        peak = jnp.max(peaks, axis=0, keepdims=True)
        total = jnp.sum(totals * jnp.exp(peaks - peak), axis=0, keepdims=True)
        picked = jnp.sum(chosen, axis=0, keepdims=True)
        log_total = peak + jnp.log(total)
        loss = jnp.broadcast_to(log_total - picked, (8, padded))
        lossb[h] = pltpu.roll(loss, lax.rem((h - p) * chunk + nP * padded, padded), axis=1)
        softmax = jnp.exp(acc[h] - to_column(log_total)[:tokens])
        dl[h] = (of_chunk(scale_col, h) * (softmax - hits(h).astype(f32))).astype(bf16)

    def pick(step, values):
        out = jnp.int32(values[0])
        for n in range(1, len(values)):
            if values[n] != values[n - 1]:
                out = out + jnp.where(step >= n, values[n] - values[n - 1], 0)
        return out

    def order(step):
        return pick(step, [h for h, _ in turns_]), near(pick(step, [i for _, i in turns_]))

    def produce(step):
        h, k = order(step)
        for b_ in range(nB):
            tt = k * nB + b_
            for part in (pl.ds(0, cols // 2), pl.ds(cols // 2, cols // 2)):
                term = jnp.dot(dl[h], WT[tt, :, part], preferred_element_type=f32)
                Pb[h, tt, :, :, :, part] = term.reshape(nA, 2, chunk, cols // 2)
            put(Pb.at[h, tt, :, 1 - c], Sib.at[h, tt], 1, gs.at[h, k], sib)

    def stage1(step):
        h, k = order(step)
        got(Sib.at[h, pl.ds(0, nB)], gs.at[h, k])
        for b_ in range(nB):
            for a_ in range(nA):
                Sib[h, k * nB + b_, a_] = Sib[h, k * nB + b_, a_] + Pb[h, k * nB + b_, a_, c]
        for o in range(1, nA):
            at_, to = (o - 1) * nB, (nA - o - 1) * nB
            for b_ in range(nB):
                b1[h, k, at_ + b_] = Sib[h, k * nB + b_, As[o - 1], :, lo].astype(bf16)
            put(
                b1.at[h, k, pl.ds(at_, nB)], r1.at[h, k, pl.ds(to, nB)],
                2, g1.at[h, k], at(a_=As[o - 1]),
            )
        for o in range(1, nB):
            at_, to = base + (o - 1) * nA, base + (nB - o - 1) * nA
            for a_ in range(nA):
                b1[h, k, at_ + a_] = Sib[h, k * nB + Bs[o - 1], a_, :, hi].astype(bf16)
            put(
                b1.at[h, k, pl.ds(at_, nA)], r1.at[h, k, pl.ds(to, nA)],
                2, g1.at[h, k], at(b_=Bs[o - 1]),
            )

    base, turned = (nA - 1) * nB, nB - 1

    def from_x(h, k, j):
        return sum(r1[h, k, m * nB + j].astype(f32) for m in range(nA - 1))

    def from_y(h, k, j):
        return sum(r1[h, k, base + m * nA + j].astype(f32) for m in range(nB - 1))

    def stage2(step):
        h, k = order(step)
        tb = k * nB + b
        got(r1.at[h, k], g1.at[h, k])
        for o in range(1, nB):
            j = Bs[o - 1]
            b2[h, k, o - 1] = (Sib[h, k * nB + j, a, :, lo] + from_x(h, k, j)).astype(bf16)
            put(b2.at[h, k, o - 1], r2.at[h, k, nB - o - 1], 3, gd.at[h, k], at(b_=j))
        for o in range(1, nA):
            j = As[o - 1]
            b2[h, k, turned + o - 1] = (Sib[h, tb, j, :, hi] + from_y(h, k, j)).astype(bf16)
            put(
                b2.at[h, k, turned + o - 1], r2.at[h, k, turned + nA - o - 1],
                3, gd.at[h, k], at(a_=j),
            )
        Sib[h, tb, a, :, lo] = Sib[h, tb, a, :, lo] + from_x(h, k, b)
        Sib[h, tb, a, :, hi] = Sib[h, tb, a, :, hi] + from_y(h, k, a)

    def stage3(step):
        h, k = order(step)
        tb = k * nB + b
        got(r2.at[h, k], gd.at[h, k])
        low = Sib[h, tb, a, :, lo] + sum(r2[h, k, m].astype(f32) for m in range(turned))
        high = Sib[h, tb, a, :, hi] + sum(
            r2[h, k, turned + m].astype(f32) for m in range(nA - 1)
        )

        @pl.when(k != z)
        def _():
            zb[h, k, :, lo] = low.astype(bf16)
            zb[h, k, :, hi] = high.astype(bf16)
            put(zb.at[h, k], zr.at[h, z], 4, rz.at[h], at(z_=k))

        @pl.when(k == z)
        def _():
            keep[h, :, lo] = low
            keep[h, :, hi] = high

    def complete(h):
        got(zr.at[h, pl.ds(0, nC - 1)], rz.at[h])
        keep[h] = keep[h] + sum(zr[h, k].astype(f32) for k in Zs)
        pltpu.make_async_copy(keep.at[h], grad_out.at[pl.ds(h * chunk, chunk)], osem.at[h]).start()

    nF, nS = nH * (nC - 1), nH * nC
    turns_ = [(h, nC - 1 - i) for h in range(nH) for i in range(nC)]
    later = list(range(nH))
    if nH == 3 and nC == 4:
        turns_ = [(0, i) for i in (3, 2, 1, 0)] + [(1, i) for i in (3, 2, 1)]
        turns_ += [(2, i) for i in (3, 2, 1)] + [(1, 0), (2, 0)]
        later = (0, 1, 1)
    B = 1 if nH > 1 else 0
    o2 = 2
    c0 = B + nC - 2 + 2 + 2 + 0
    begin = c0 + 2 + 0
    comm, work, stats, back = [], [], [], []
    add = lambda to, when, action, *args: to.append((when, None, action, args))
    own = lambda h: h if h < 2 else o2 + (h - 2) * nC
    for h in range(2, nH):
        if not False:
            add(comm, own(h) - 2, own_plane, h)
    for h in range(nH):
        add(comm, own(h), own_forward, h)
    for h in range(1, nH):
        add(comm, 1 + (h - 1) * 4, own_line, h, 0)
    comm.append((B, nF, spread, ()))
    comm.append((B + 2, nF, forward, ()))
    for h in range(nH):
        add(comm, own(h) + 2, own_finish, h)
    comm.append((B + 2 + 2, nF, finish, ()))
    for h in range(nH):
        add(work, own(h) + 2 + 1, own_multiply, h)
    work.append((B + 2 + 2 + 0, nF, multiply, ()))
    share = min(n for n in range(1, nT + 1) if nT % n == 0 and 1 + nT // n <= begin)
    turning = [(1, nT // share, turn, ())]
    add(comm, 0, wcopy.wait)
    for h in range(nH):
        w = c0 + h * (nC - 1)
        add(stats, w + 2 + later[h], stats_line, h)
        add(work, w, stats_local, h)
    back += [(begin + 1, nS, stage1, ()), (begin + 1 + 2, nS, stage2, ()), (begin + 1 + 2 + 2, nS, stage3, ()), (begin, nS, produce, ())]
    end = 1 + 2 + 2
    for h in range(nH):
        at_ = turns_.index((h, 0)) + (2 if h < nH - 1 else 0)
        add(back, begin + min(at_, nS - 1) + end, complete, h)
    plans = [comm, turning, stats, back, work]
    length = begin + nS + end

    with jax.named_scope("barrier"):
        pl.semaphore_wait(barrier, len(peers))
    own_plane(0)
    own_line(0, 1)
    for copy in [tcopy, kcopy] + hcopies + [wcopy]:
        copy.start()
    with jax.named_scope("zero"):
        acc[...] = jnp.zeros_like(acc)
        tcopy.wait()
        kcopy.wait()
        target_col = to_column(tbuf[...].reshape(1, -1).astype(f32)).astype(jnp.int32)
        scale_col = loss_scale * to_column(wbuf[...].reshape(1, -1))
    own_line(0, 2)
    if nH > 1:
        own_plane(1)

    def during(i, begin, count, action):
        @pl.when((i >= begin) & (i < begin + count))
        def _():
            with jax.named_scope(action.__name__):
                action(i - begin)

    def once(i, when, action, *args):
        @pl.when(i == when)
        def _():
            with jax.named_scope(action.__name__):
                action(*args)

    def step(i, carry):
        for entries in plans:
            first_i = min(e[0] for e in entries)
            last_i = max(e[0] + (e[1] or 1) for e in entries)

            @pl.when((i >= first_i) & (i < last_i))
            def _():
                for when, count, action, args in entries:
                    if count is None:
                        once(i, when, action, *args)
                    else:
                        during(i, when, count, action)
        return carry

    lax.fori_loop(0, length, step, 0)
    with jax.named_scope("loss"):
        lane = lax.broadcasted_iota(jnp.int32, (8, padded), 1)
        loss = lossb[0]
        for h in range(1, nH):
            loss = jnp.where(lane >= h * chunk, lossb[h], loss)
        lossrow[...] = loss[0, :rows]
        lcopy = pltpu.make_async_copy(lossrow, loss_out, lsem.at[1])
        lcopy.start()

    with jax.named_scope('drain'):
        sent(blocks(nH * (nT * nP - 1)), 0)
        sent(Sib, 1)
        sent(b1, 2)
        sent(b2, 3)
        sent(zb.at[:, pl.ds(0, nC - 1)], 4)
        sent(st.at[:, pl.ds(0, len(Everyone))], 5)
        for h in range(nH):
            pltpu.make_async_copy(keep.at[h], grad_out.at[pl.ds(h * chunk, chunk)], osem.at[h]).wait()
        lcopy.wait()


def hand_over(loss, grad, loss_out, grad_out):
    loss_out[...] = loss[...]
    grad_out[...] = grad[...]


def local(hidden, weight, targets, token_weight):
    rows, cols = hidden.shape
    n_pipe, n_tensor = lax.axis_size("pipe"), lax.axis_size("tensor")
    nA, nB, nC = n_pipe // 2, 2, n_tensor // 2
    tokens, width = targets.shape[0], weight.shape[1]
    vmem, dma = pltpu.VMEM, pltpu.SemaphoreType.DMA
    nH = 3 if rows % (16 * 3) == 0 else 1
    chunk = rows // nH
    half = cols // 2
    n1, n2 = (nA - 1) * nB + (nB - 1) * nA, nB + nA - 2
    part = n_pipe * chunk
    padded = -(-part // 128) * 128
    token_loss, hidden_grad = pl.pallas_call(
        functools.partial(kernel, nA, nB, nC, nH),
        out_shape=(
            jax.ShapeDtypeStruct((rows,), f32),
            jax.ShapeDtypeStruct((rows, cols), f32),
        ),
        in_specs=[pl.BlockSpec(memory_space=pl.ANY)] * 4,
        out_specs=[pl.BlockSpec(memory_space=pl.ANY)] * 2,
        scratch_shapes=[
            vmem((nH * n_tensor * n_pipe, chunk, cols), bf16),
            vmem((n_tensor, cols, width), bf16),
            vmem((n_tensor, width, cols), bf16),
            vmem((nH, part, width), f32),
            vmem((nH, part, width), bf16),
            vmem((nH, n_tensor, nA, 2, chunk, cols), f32),
            vmem((nH, n_tensor, nA, chunk, cols), f32),
            vmem((nH, nC, n1, chunk, half), bf16),
            vmem((nH, nC, n1, chunk, half), bf16),
            vmem((nH, nC, n2, chunk, half), bf16),
            vmem((nH, nC, n2, chunk, half), bf16),
            vmem((nH, nC, chunk, cols), bf16),
            vmem((nH, nC, chunk, cols), bf16),
            vmem((nH, chunk, cols), f32),
            vmem((nH, 8, padded), f32),
            vmem((nH, n_pipe * n_tensor, 4, padded), f32),
            vmem((nH, 8, padded), f32),
            vmem((rows,), f32),
            vmem((tokens,), jnp.int32),
            vmem((tokens,), f32),
            dma((3,)),
            dma((nH,)),
            dma((nH,)),
            dma((6,)),
            dma((nH, nC)),
            dma((nH, nC)),
            dma((nH, nC)),
            dma((nH, nC)),
            dma((nH,)),
            dma((nH,)),
        ],
        compiler_params=pltpu.CompilerParams(
            collective_id=0, has_side_effects=True, vmem_limit_bytes=52 * 1024 * 1024
        ),
    )(
        pltpu.with_memory_space_constraint(hidden, pltpu.HBM),
        weight.reshape(n_tensor, cols, width),
        pltpu.with_memory_space_constraint(targets, pltpu.HBM),
        pltpu.with_memory_space_constraint(token_weight, pltpu.HBM),
    )
    return pl.pallas_call(
        hand_over,
        out_shape=(
            jax.ShapeDtypeStruct((rows,), f32),
            jax.ShapeDtypeStruct((rows, cols), f32),
        ),
        in_specs=[pl.BlockSpec(memory_space=vmem)] * 2,
        out_specs=[pl.BlockSpec(memory_space=vmem)] * 2,

        compiler_params=pltpu.CompilerParams(vmem_limit_bytes=4 * 1024 * 1024),
    )(token_loss, hidden_grad)


def solution(mesh):
    in_specs = (P("pipe", "tensor"), P(None, ("pipe", "tensor")), P(), P())
    out_specs = (P("pipe"), P("pipe", "tensor"))
    return jax.shard_map(local, mesh=mesh, in_specs=in_specs, out_specs=out_specs, check_vma=False)
```

```python
import functools

import jax
import jax.numpy as jnp
from jax import lax
from jax.experimental import pallas as pl
from jax.experimental.pallas import tpu as pltpu
from jax.sharding import PartitionSpec as P

loss_scale = 32.0
f32, bf16 = jnp.float32, jnp.bfloat16
MESH = pl.DeviceIdType.MESH


def flat_rows(block):
    n, rows, width = block.shape
    if rows % 16:
        return block.astype(f32).reshape(n * rows, width).astype(bf16)
    return block.reshape(n * rows, width)


def to_column(row):
    return jnp.transpose(jnp.broadcast_to(row, (128, row.shape[1])))[:, :1]


def kernel(
    nA, nB, nC, nH,
    hidden, weight, targets, token_weight,
    loss_out, grad_out,
    H, W, WT, acc, dl, Pb, Sib, b1, r1, b2, r2, zb, zr, keep, stb, st, lossb, lossrow, tbuf, wbuf,
    lsem, hsem, osem, sends, g1, gd, gs, gz, rz, ssem,
):
    rows, cols = hidden.shape
    chunk = rows // nH
    half = cols // 2
    nP, nT = nA * 2, nB * nC
    lo, hi = pl.ds(0, half), pl.ds(half, half)
    p, t = lax.axis_index("pipe"), lax.axis_index("tensor")
    a, c = p // 2, lax.rem(p, 2)
    b, z = lax.rem(t, nB), t // nB

    def at(a_=None, b_=None, z_=None, c_=None):
        a_, b_ = (a if a_ is None else a_), (b if b_ is None else b_)
        z_, c_ = (z if z_ is None else z_), (c if c_ is None else c_)
        return {"pipe": a_ * 2 + c_, "tensor": z_ * nB + b_}

    left, right = z, nC - 1 - z
    both = jnp.minimum(left, right)
    longer = jnp.where(left > right, -1, 1)

    def near(i):
        d = (i + 1) // 2
        turn = jnp.where(lax.rem(i, 2) == 1, -d, d)
        return z + jnp.where(i <= 2 * both, turn, longer * (i - both))

    As = [lax.rem(a + o, nA) for o in range(1, nA)]
    Bs = [lax.rem(b + o, nB) for o in range(1, nB)]
    Zs = [near(jnp.int32(i)) for i in range(1, nC)]
    sib = at(c_=1 - c)
    Everyone = [
        at(a_=a_, b_=b_, c_=c_, z_=z_)
        for z_ in [z] + Zs for a_ in [a] + As for b_ in [b] + Bs for c_ in (c, 1 - c)
    ][1:]
    peers = Everyone[: nP * nB - 1] + [at(z_=k) for k in Zs]

    def put(src, dst, send, recv, dev):
        pltpu.make_async_remote_copy(
            src_ref=src, dst_ref=dst, send_sem=sends.at[send], recv_sem=recv,
            device_id=dev, device_id_type=MESH,
        ).start()

    def got(dst, recv):
        pltpu.make_async_remote_copy(
            src_ref=dst, dst_ref=dst, send_sem=sends.at[0], recv_sem=recv,
            device_id=sib, device_id_type=MESH,
        ).wait_recv()

    def sent(src, send):
        pltpu.make_async_remote_copy(
            src_ref=src, dst_ref=src, send_sem=sends.at[send], recv_sem=rz.at[0],
            device_id=sib, device_id_type=MESH,
        ).wait_send()

    barrier = pltpu.get_barrier_semaphore()
    for dev in peers:
        pl.semaphore_signal(barrier, inc=1, device_id=dev, device_id_type=MESH)

    def where(h, k, b_, a_, c_=None):
        return (h * nT + k * nB + b_) * nP + a_ * 2 + (c if c_ is None else c_)

    def slot(h, k, b_, a_):
        return H.at[where(h, k, b_, a_)]

    def blocks(n):
        return H.at[pl.ds(0, n)]

    hcopies = [
        pltpu.make_async_copy(
            hidden.at[pl.ds(h * chunk, chunk)], slot(h, z, b, a), hsem.at[h]
        )
        for h in range(nH)
    ]
    tcopy = pltpu.make_async_copy(targets, tbuf, lsem.at[1])
    kcopy = pltpu.make_async_copy(token_weight, wbuf, lsem.at[2])
    wcopy = pltpu.make_async_copy(weight, W, lsem.at[0])

    def own_plane(h):
        src, own = hidden.at[pl.ds(h * chunk, chunk)], slot(h, z, b, a)
        for j in As:
            put(src, own, 0, g1.at[h, z], at(a_=j))
        for j in Bs:
            put(src, own, 0, g1.at[h, z], at(b_=j))
        put(src, own, 0, gs.at[h, z], sib)

    def own_line(h, group):
        src, own = hidden.at[pl.ds(h * chunk, chunk)], slot(h, z, b, a)
        for k in (Zs, Zs[:2], Zs[2:])[group]:
            put(src, own, 0, gz.at[h, z], at(z_=k))

    def turn(n):
        for m in range(share):
            WT[n * share + m] = jnp.transpose(W[n * share + m])

    def diagonal(h, k):
        for j in As:
            for m in Bs:
                ref = slot(h, k, b, j).at[:, lo]
                put(ref, ref, 0, gd.at[h, k], at(b_=m))
        for j in Bs:
            for m in As:
                ref = slot(h, k, j, a).at[:, hi]
                put(ref, ref, 0, gd.at[h, k], at(a_=m))

    def sibling(h, k, places):
        for b_, a_ in places:
            put(slot(h, k, b_, a_), slot(h, k, b_, a_), 0, gs.at[h, k], sib)

    beside = [(b, j) for j in As] + [(j, a) for j in Bs]
    across = [(m, j) for j in As for m in Bs]

    def own_forward(h):
        got(blocks(len(beside)), g1.at[h, z])
        diagonal(h, z)
        sibling(h, z, beside)

    def own_finish(h):
        got(blocks(len(across)), gd.at[h, z])
        sibling(h, z, across)

    def far(step):
        return step // (nC - 1), near(lax.rem(step, nC - 1) + 1)

    def spread(step):
        h, k = far(step)
        own = slot(h, k, b, a)
        got(own, gz.at[h, k])
        for j in As:
            put(own, own, 0, g1.at[h, k], at(a_=j))
        for j in Bs:
            put(own, own, 0, g1.at[h, k], at(b_=j))
        put(own, own, 0, gs.at[h, k], sib)

    def forward(step):
        h, k = far(step)
        got(blocks(len(beside)), g1.at[h, k])
        diagonal(h, k)
        sibling(h, k, beside)

    def finish(step):
        h, k = far(step)
        got(blocks(len(across)), gd.at[h, k])
        sibling(h, k, across)

    def product(h, k):
        got(blocks(nA * nB), gs.at[h, k])
        for b_ in range(nB):
            tt = k * nB + b_
            lhs = flat_rows(H[pl.ds((h * nT + tt) * nP, nP)])
            acc[h] += jnp.dot(lhs, W[tt], preferred_element_type=f32)

    def multiply(step):
        product(*far(step))

    def own_multiply(h):
        hcopies[h].wait()
        product(h, z)

    tokens, width = acc.shape[1:]
    padded = stb.shape[-1]
    device_block = p * lax.axis_size("tensor") + t
    def of_chunk(column, h):
        return column.reshape(nP, nH, chunk, 1)[:, h].reshape(nP * chunk, 1)

    def hits(h):
        columns = device_block * width + lax.broadcasted_iota(jnp.int32, (tokens, width), 1)
        return of_chunk(target_col, h) == columns

    def stats_local(h):
        logits = acc[h]
        peak = jnp.max(logits, axis=1, keepdims=True)
        total = jnp.sum(jnp.exp(logits - peak), axis=1, keepdims=True)
        chosen = jnp.sum(jnp.where(hits(h), logits, 0.0), axis=1, keepdims=True)
        lane = lax.broadcasted_iota(jnp.int32, (tokens, 128), 1)
        packed = jnp.where(
            lane == 0, peak, jnp.where(lane == 1, total, jnp.where(lane == 2, chosen, 0.0))
        )
        if padded > tokens:
            packed = jnp.concatenate([packed, jnp.zeros((padded - tokens, 128), f32)], axis=0)
        stb[h] = jnp.transpose(packed)[0:8]
        for dev in Everyone:
            put(stb.at[h, pl.ds(0, 4)], st.at[h, device_block], 5, ssem.at[h], dev)
        st[h, device_block] = stb[h, 0:4]

    def stats_line(h):
        got(st.at[h, pl.ds(0, len(Everyone))], ssem.at[h])
        peaks, totals, chosen = (st[h, :, n : n + 1].reshape(len(Everyone) + 1, padded) for n in range(3))
        peak = jnp.max(peaks, axis=0, keepdims=True)
        total = jnp.sum(totals * jnp.exp(peaks - peak), axis=0, keepdims=True)
        picked = jnp.sum(chosen, axis=0, keepdims=True)
        log_total = peak + jnp.log(total)
        loss = jnp.broadcast_to(log_total - picked, (8, padded))
        lossb[h] = pltpu.roll(loss, lax.rem((h - p) * chunk + nP * padded, padded), axis=1)
        softmax = jnp.exp(acc[h] - to_column(log_total)[:tokens])
        dl[h] = (of_chunk(scale_col, h) * (softmax - hits(h).astype(f32))).astype(bf16)

    def pick(step, values):
        out = jnp.int32(values[0])
        for n in range(1, len(values)):
            if values[n] != values[n - 1]:
                out = out + jnp.where(step >= n, values[n] - values[n - 1], 0)
        return out

    def order(step):
        return pick(step, [h for h, _ in turns_]), near(pick(step, [i for _, i in turns_]))

    def produce(step):
        h, k = order(step)
        for b_ in range(nB):
            tt = k * nB + b_
            for part in (pl.ds(0, cols // 2), pl.ds(cols // 2, cols // 2)):
                term = jnp.dot(dl[h], WT[tt, :, part], preferred_element_type=f32)
                Pb[h, tt, :, :, :, part] = term.reshape(nA, 2, chunk, cols // 2)
            put(Pb.at[h, tt, :, 1 - c], Sib.at[h, tt], 1, gs.at[h, k], sib)

    def stage1(step):
        h, k = order(step)
        got(Sib.at[h, pl.ds(0, nB)], gs.at[h, k])
        for b_ in range(nB):
            for a_ in range(nA):
                Sib[h, k * nB + b_, a_] = Sib[h, k * nB + b_, a_] + Pb[h, k * nB + b_, a_, c]
        for o in range(1, nA):
            at_, to = (o - 1) * nB, (nA - o - 1) * nB
            for b_ in range(nB):
                b1[h, k, at_ + b_] = Sib[h, k * nB + b_, As[o - 1], :, lo].astype(bf16)
            put(
                b1.at[h, k, pl.ds(at_, nB)], r1.at[h, k, pl.ds(to, nB)],
                2, g1.at[h, k], at(a_=As[o - 1]),
            )
        for o in range(1, nB):
            at_, to = base + (o - 1) * nA, base + (nB - o - 1) * nA
            for a_ in range(nA):
                b1[h, k, at_ + a_] = Sib[h, k * nB + Bs[o - 1], a_, :, hi].astype(bf16)
            put(
                b1.at[h, k, pl.ds(at_, nA)], r1.at[h, k, pl.ds(to, nA)],
                2, g1.at[h, k], at(b_=Bs[o - 1]),
            )

    base, turned = (nA - 1) * nB, nB - 1

    def from_x(h, k, j):
        return sum(r1[h, k, m * nB + j].astype(f32) for m in range(nA - 1))

    def from_y(h, k, j):
        return sum(r1[h, k, base + m * nA + j].astype(f32) for m in range(nB - 1))

    def stage2(step):
        h, k = order(step)
        tb = k * nB + b
        got(r1.at[h, k], g1.at[h, k])
        for o in range(1, nB):
            j = Bs[o - 1]
            b2[h, k, o - 1] = (Sib[h, k * nB + j, a, :, lo] + from_x(h, k, j)).astype(bf16)
            put(b2.at[h, k, o - 1], r2.at[h, k, nB - o - 1], 3, gd.at[h, k], at(b_=j))
        for o in range(1, nA):
            j = As[o - 1]
            b2[h, k, turned + o - 1] = (Sib[h, tb, j, :, hi] + from_y(h, k, j)).astype(bf16)
            put(
                b2.at[h, k, turned + o - 1], r2.at[h, k, turned + nA - o - 1],
                3, gd.at[h, k], at(a_=j),
            )
        Sib[h, tb, a, :, lo] = Sib[h, tb, a, :, lo] + from_x(h, k, b)
        Sib[h, tb, a, :, hi] = Sib[h, tb, a, :, hi] + from_y(h, k, a)

    def stage3(step):
        h, k = order(step)
        tb = k * nB + b
        got(r2.at[h, k], gd.at[h, k])
        low = Sib[h, tb, a, :, lo] + sum(r2[h, k, m].astype(f32) for m in range(turned))
        high = Sib[h, tb, a, :, hi] + sum(
            r2[h, k, turned + m].astype(f32) for m in range(nA - 1)
        )

        @pl.when(k != z)
        def _():
            zb[h, k, :, lo] = low.astype(bf16)
            zb[h, k, :, hi] = high.astype(bf16)
            put(zb.at[h, k], zr.at[h, z], 4, rz.at[h], at(z_=k))

        @pl.when(k == z)
        def _():
            keep[h, :, lo] = low
            keep[h, :, hi] = high

    def complete(h):
        got(zr.at[h, pl.ds(0, nC - 1)], rz.at[h])
        keep[h] = keep[h] + sum(zr[h, k].astype(f32) for k in Zs)
        pltpu.make_async_copy(keep.at[h], grad_out.at[pl.ds(h * chunk, chunk)], osem.at[h]).start()

    nF, nS = nH * (nC - 1), nH * nC
    turns_ = [(h, nC - 1 - i) for h in range(nH) for i in range(nC)]
    later = list(range(nH))
    if nH == 3 and nC == 4:
        turns_ = [(0, i) for i in (3, 2, 1, 0)] + [(1, i) for i in (3, 2, 1)]
        turns_ += [(2, i) for i in (3, 2, 1)] + [(1, 0), (2, 0)]
        later = (0, 1, 1)
    B = 1 if nH > 1 else 0
    o2 = 2
    c0 = B + nC - 2 + 2 + 2 + 0
    begin = c0 + 2 + 0
    comm, work, stats, back = [], [], [], []
    add = lambda to, when, action, *args: to.append((when, None, action, args))
    own = lambda h: h if h < 2 else o2 + (h - 2) * nC
    for h in range(2, nH):
        if not False:
            add(comm, own(h) - 2, own_plane, h)
    for h in range(nH):
        add(comm, own(h), own_forward, h)
    for h in range(1, nH):
        add(comm, 1 + (h - 1) * 4, own_line, h, 1)
        add(comm, 1 + 1 + (h - 1) * 4, own_line, h, 2)
    comm.append((B, nF, spread, ()))
    comm.append((B + 2, nF, forward, ()))
    for h in range(nH):
        add(comm, own(h) + 2, own_finish, h)
    comm.append((B + 2 + 2, nF, finish, ()))
    for h in range(nH):
        add(work, own(h) + 2 + 1, own_multiply, h)
    work.append((B + 2 + 2 + 0, nF, multiply, ()))
    share = min(n for n in range(1, nT + 1) if nT % n == 0 and 1 + nT // n <= begin)
    turning = [(1, nT // share, turn, ())]
    add(comm, 0, wcopy.wait)
    for h in range(nH):
        w = c0 + h * (nC - 1)
        add(stats, w + 2 + later[h], stats_line, h)
        add(work, w, stats_local, h)
    back += [(begin + 1, nS, stage1, ()), (begin + 1 + 2, nS, stage2, ()), (begin + 1 + 2 + 2, nS, stage3, ()), (begin, nS, produce, ())]
    end = 1 + 2 + 2
    for h in range(nH):
        at_ = turns_.index((h, 0)) + (2 if h < nH - 1 else 0)
        add(back, begin + min(at_, nS - 1) + end, complete, h)
    plans = [comm, turning, stats, back, work]
    length = begin + nS + end

    with jax.named_scope("barrier"):
        pl.semaphore_wait(barrier, len(peers))
    own_plane(0)
    own_line(0, 1)
    for copy in [tcopy, kcopy] + hcopies + [wcopy]:
        copy.start()
    with jax.named_scope("zero"):
        acc[...] = jnp.zeros_like(acc)
        tcopy.wait()
        kcopy.wait()
        target_col = to_column(tbuf[...].reshape(1, -1).astype(f32)).astype(jnp.int32)
        scale_col = loss_scale * to_column(wbuf[...].reshape(1, -1))
    own_line(0, 2)
    if nH > 1:
        own_plane(1)

    def during(i, begin, count, action):
        @pl.when((i >= begin) & (i < begin + count))
        def _():
            with jax.named_scope(action.__name__):
                action(i - begin)

    def once(i, when, action, *args):
        @pl.when(i == when)
        def _():
            with jax.named_scope(action.__name__):
                action(*args)

    def step(i, carry):
        for entries in plans:
            first_i = min(e[0] for e in entries)
            last_i = max(e[0] + (e[1] or 1) for e in entries)

            @pl.when((i >= first_i) & (i < last_i))
            def _():
                for when, count, action, args in entries:
                    if count is None:
                        once(i, when, action, *args)
                    else:
                        during(i, when, count, action)
        return carry

    lax.fori_loop(0, length, step, 0)
    with jax.named_scope("loss"):
        lane = lax.broadcasted_iota(jnp.int32, (8, padded), 1)
        loss = lossb[0]
        for h in range(1, nH):
            loss = jnp.where(lane >= h * chunk, lossb[h], loss)
        lossrow[...] = loss[0, :rows]
        lcopy = pltpu.make_async_copy(lossrow, loss_out, lsem.at[1])
        lcopy.start()

    with jax.named_scope('drain'):
        sent(blocks(nH * (nT * nP - 1)), 0)
        sent(Sib, 1)
        sent(b1, 2)
        sent(b2, 3)
        sent(zb.at[:, pl.ds(0, nC - 1)], 4)
        sent(st.at[:, pl.ds(0, len(Everyone))], 5)
        for h in range(nH):
            pltpu.make_async_copy(keep.at[h], grad_out.at[pl.ds(h * chunk, chunk)], osem.at[h]).wait()
        lcopy.wait()


def hand_over(loss, grad, loss_out, grad_out):
    loss_out[...] = loss[...]
    grad_out[...] = grad[...]


def local(hidden, weight, targets, token_weight):
    rows, cols = hidden.shape
    n_pipe, n_tensor = lax.axis_size("pipe"), lax.axis_size("tensor")
    nA, nB, nC = n_pipe // 2, 2, n_tensor // 2
    tokens, width = targets.shape[0], weight.shape[1]
    vmem, dma = pltpu.VMEM, pltpu.SemaphoreType.DMA
    nH = 3 if rows % (16 * 3) == 0 else 1
    chunk = rows // nH
    half = cols // 2
    n1, n2 = (nA - 1) * nB + (nB - 1) * nA, nB + nA - 2
    part = n_pipe * chunk
    padded = -(-part // 128) * 128
    token_loss, hidden_grad = pl.pallas_call(
        functools.partial(kernel, nA, nB, nC, nH),
        out_shape=(
            jax.ShapeDtypeStruct((rows,), f32),
            jax.ShapeDtypeStruct((rows, cols), f32),
        ),
        in_specs=[pl.BlockSpec(memory_space=pl.ANY)] * 4,
        out_specs=[pl.BlockSpec(memory_space=pl.ANY)] * 2,
        scratch_shapes=[
            vmem((nH * n_tensor * n_pipe, chunk, cols), bf16),
            vmem((n_tensor, cols, width), bf16),
            vmem((n_tensor, width, cols), bf16),
            vmem((nH, part, width), f32),
            vmem((nH, part, width), bf16),
            vmem((nH, n_tensor, nA, 2, chunk, cols), f32),
            vmem((nH, n_tensor, nA, chunk, cols), f32),
            vmem((nH, nC, n1, chunk, half), bf16),
            vmem((nH, nC, n1, chunk, half), bf16),
            vmem((nH, nC, n2, chunk, half), bf16),
            vmem((nH, nC, n2, chunk, half), bf16),
            vmem((nH, nC, chunk, cols), bf16),
            vmem((nH, nC, chunk, cols), bf16),
            vmem((nH, chunk, cols), f32),
            vmem((nH, 8, padded), f32),
            vmem((nH, n_pipe * n_tensor, 4, padded), f32),
            vmem((nH, 8, padded), f32),
            vmem((rows,), f32),
            vmem((tokens,), jnp.int32),
            vmem((tokens,), f32),
            dma((3,)),
            dma((nH,)),
            dma((nH,)),
            dma((6,)),
            dma((nH, nC)),
            dma((nH, nC)),
            dma((nH, nC)),
            dma((nH, nC)),
            dma((nH,)),
            dma((nH,)),
        ],
        compiler_params=pltpu.CompilerParams(
            collective_id=0, has_side_effects=True, vmem_limit_bytes=52 * 1024 * 1024
        ),
    )(
        pltpu.with_memory_space_constraint(hidden, pltpu.HBM),
        weight.reshape(n_tensor, cols, width),
        pltpu.with_memory_space_constraint(targets, pltpu.HBM),
        pltpu.with_memory_space_constraint(token_weight, pltpu.HBM),
    )
    return pl.pallas_call(
        hand_over,
        out_shape=(
            jax.ShapeDtypeStruct((rows,), f32),
            jax.ShapeDtypeStruct((rows, cols), f32),
        ),
        in_specs=[pl.BlockSpec(memory_space=vmem)] * 2,
        out_specs=[pl.BlockSpec(memory_space=vmem)] * 2,

        compiler_params=pltpu.CompilerParams(vmem_limit_bytes=4 * 1024 * 1024),
    )(token_loss, hidden_grad)


def solution(mesh):
    in_specs = (P("pipe", "tensor"), P(None, ("pipe", "tensor")), P(), P())
    out_specs = (P("pipe"), P("pipe", "tensor"))
    return jax.shard_map(local, mesh=mesh, in_specs=in_specs, out_specs=out_specs, check_vma=False)
```
